32 devices in a mesh: dp: 8 (over y, x, core), tensor: 4 (over z).
Axes of the slice: x: 2, y: 2, z: 4, core: 2. Of those that a mesh axis runs over, the one named last changes fastest.
Arguments:
- layer_in: bfloat16 [8192, 2048], P(('dp', 'tensor')), may hold values from -6 to 6
- w_query: bfloat16 [2048, 2048], P('dp', 'tensor'), may hold values from -0.125 to 0.125
- w_key: bfloat16 [2048, 1024], P('dp', 'tensor'), may hold values from -0.125 to 0.125
- w_value: bfloat16 [2048, 1024], P('dp', 'tensor'), may hold values from -0.125 to 0.125
- w_output: bfloat16 [2048, 2048], P('tensor', 'dp'), may hold values from -1 to 1
- w_gate_up: bfloat16 [2048, 2, 6144], P('dp', None, 'tensor'), may hold values from -0.125 to 0.125
- w_down: bfloat16 [6144, 2048], P('tensor', 'dp'), may hold values from -0.15625 to 0.15625
- pre_gain: bfloat16 [2048], P('dp'), may hold values from 0.5 to 2
- mid_gain: bfloat16 [2048], P('dp'), may hold values from 0.5 to 2
- query_gain: bfloat16 [128], P('dp'), may hold values from 0.5 to 2.5
- key_gain: bfloat16 [128], P('dp'), may hold values from 0.5 to 2.5
- out_grad: bfloat16 [8192, 2048], P(('dp', 'tensor')), may hold values from -6 to 6
Outputs:
- layer_out: bfloat16 [8192, 2048], P(('dp', 'tensor'))
- in_grad: bfloat16 [8192, 2048], P(('dp', 'tensor'))
- grad_query: float32 [2048, 2048], P('dp', 'tensor')
- grad_key: float32 [2048, 1024], P('dp', 'tensor')
- grad_value: float32 [2048, 1024], P('dp', 'tensor')
- grad_output: float32 [2048, 2048], P('tensor', 'dp')
- grad_gate_up: float32 [2048, 2, 6144], P('dp', None, 'tensor')
- grad_down: float32 [6144, 2048], P('tensor', 'dp')
- grad_pre: float32 [2048], P('dp')
- grad_mid: float32 [2048], P('dp')
- grad_qgain: float32 [128], P('dp')
- grad_kgain: float32 [128], P('dp')
The draws below stay inside these ranges and needn't reach their ends.
All inputs are finite; a program needn't handle non-finite values.
Results may differ from the reference program's by a relative error of at most 0.035.
Values may be sent and summed in bfloat16 or wider, within the bound.
No kernel may reach another device: no remote copies, remote signals or barrier semaphores. Data moves between devices by JAX's collectives and lax.ppermute only.
A program may use at most 256 MiB of HBM per device.

```python
import math
import jax
import jax.numpy as jnp
from jax import lax

D = 2048
HQ = 16
KV = 8
HD = 128
FF = 6144
L = 1024
TOKENS = 8192


def raised(values, rng, source, target, shards_of, factor):
    def block_of(axis_at):
        return (jnp.arange(values.shape[axis_at]) // (values.shape[axis_at] // shards_of)).reshape((-1,) + (1,) * (values.ndim - 1 - axis_at))

    first = jax.random.permutation(rng, shards_of)[block_of(target)]
    other_side = (block_of(target) + shards_of // 2) % shards_of
    return jnp.where((block_of(source) == first) | (block_of(source) == other_side), factor * values, values)


def steps_of(stream_key, extent, shards, smallest, top_value):
    loudness, own = 1.0, jax.random.fold_in(stream_key, 6)
    for dim, blocks in shards:
        steps = jnp.exp(jax.random.uniform(jax.random.fold_in(own, dim), (blocks,), jnp.float32, smallest / len(shards), top_value / len(shards)))
        loudness = loudness * jnp.repeat(steps, extent[dim] // blocks).reshape([-1 if axis == dim else 1 for axis in range(len(extent))])
    return loudness


def centred(own_key, dims, deviation, most, pieces=(), kind=jnp.bfloat16):
    drawn = deviation * jax.random.normal(own_key, dims, jnp.float32)
    if pieces:
        drawn = drawn * steps_of(own_key, dims, pieces, -0.22, 0.18)
    return jnp.clip(drawn, -most, most).astype(kind)


def noise_with(key, shape, spread, limit, pieces, heavy, kind=jnp.bfloat16):
    array = spread * jax.random.normal(key, shape, jnp.float32)
    if pieces:
        array = array * steps_of(key, shape, pieces, -0.22, 0.18)
    return jnp.clip(raised(array, jax.random.fold_in(key, 3), *heavy), -limit, limit).astype(kind)


def setup_inputs(seed: int = 0) -> dict:
    seeds = jax.random.split(jax.random.key(seed), 13)
    layer_in = noise_with(seeds[0], (TOKENS, D), 1.0, 6.0, ((0, 32),), (0, 1, 32, 2.75))
    w_query = centred(seeds[1], (D, HQ * HD), D ** -0.5, 0.125, ((0, 8), (1, 4)))
    w_key = centred(seeds[2], (D, KV * HD), D ** -0.5, 0.125, ((0, 8), (1, 4)))
    w_value = centred(seeds[3], (D, KV * HD), D ** -0.5, 0.125, ((0, 8), (1, 4)))
    w_output = centred(seeds[4], (HQ * HD, D), (HQ * HD // 64) ** -0.5, 1.0, ((0, 4), (1, 8)))
    w_gate_up = centred(seeds[5], (D, 2, FF), D ** -0.5, 0.125, ((0, 8), (2, 4)))
    w_down = centred(seeds[6], (FF, D), (FF // 4) ** -0.5, 0.15625, ((0, 4), (1, 8)))
    pre_gain = jnp.clip(jnp.exp(math.log(2.0) - 1.3862944 * jax.random.uniform(seeds[7], (D,), jnp.float32) ** steps_of(seeds[7], (D,), ((0, 8),), -0.2, 0.2)), 0.5, 2.0).astype(jnp.bfloat16)
    mid_gain = jnp.clip(jnp.exp(math.log(2.0) - 1.3862944 * jax.random.uniform(seeds[8], (D,), jnp.float32) ** steps_of(seeds[8], (D,), ((0, 8),), -0.2, 0.2)), 0.5, 2.0).astype(jnp.bfloat16)
    query_gain = jnp.clip(jnp.exp(math.log(2.5) - 1.609438 * jax.random.uniform(seeds[9], (HD,), jnp.float32) ** steps_of(seeds[9], (HD,), ((0, 8),), -0.2, 0.2)), 0.5, 2.5).astype(jnp.bfloat16)
    key_gain = jnp.clip(jnp.exp(math.log(2.5) - 1.609438 * jax.random.uniform(seeds[10], (HD,), jnp.float32) ** steps_of(seeds[10], (HD,), ((0, 8),), -0.2, 0.2)), 0.5, 2.5).astype(jnp.bfloat16)
    out_grad = noise_with(seeds[11], (TOKENS, D), 1.0, 6.0, ((0, 32),), (0, 1, 32, 2.75))
    return dict(layer_in=layer_in, w_query=w_query, w_key=w_key, w_value=w_value, w_output=w_output, w_gate_up=w_gate_up, w_down=w_down, pre_gain=pre_gain, mid_gain=mid_gain, query_gain=query_gain, key_gain=key_gain, out_grad=out_grad)


EPS = 1e-06
THETA = 1000000.0

def contract_rows(left, right):
    return lax.dot_general(left, right, (((0,), (0,)), ((), ())), preferred_element_type=jnp.float32)

def contract_cols(left, right):
    return lax.dot_general(left, right, (((1,), (1,)), ((), ())), preferred_element_type=jnp.float32)

def rope_tables(positions, head_size):
    half = head_size // 2
    freq = THETA ** (-(jnp.arange(half, dtype=jnp.float32) * 2.0) / head_size)
    angle = positions.astype(jnp.float32)[:, None] * freq[None, :]
    cosine = jnp.concatenate([jnp.cos(angle), jnp.cos(angle)], axis=1)[:, None, :]
    sine = jnp.concatenate([jnp.sin(angle), jnp.sin(angle)], axis=1)[:, None, :]
    return (cosine, sine)

def rotate(values, cosine, sine):
    half = values.shape[-1] // 2
    turned = jnp.concatenate([-values[..., half:], values[..., :half]], axis=-1)
    return values * cosine + turned * sine

def unrotate(grads, cosine, sine):
    half = grads.shape[-1] // 2
    scaled = grads * sine
    back = jnp.concatenate([scaled[..., half:], -scaled[..., :half]], axis=-1)
    return grads * cosine + back

def rms_forward(values, gain):
    scale = lax.rsqrt(lax.optimization_barrier(jnp.mean(values * values, axis=-1, keepdims=True)) + EPS)
    return (values * scale * gain, scale)

def rms_back(values, scale, gain, grads):
    normal = values * scale
    scaled = grads * gain
    inner = lax.optimization_barrier(jnp.mean(scaled * normal, axis=-1, keepdims=True))
    back = scale * (scaled - normal * inner)
    gain_part = lax.optimization_barrier(jnp.sum((grads * normal).reshape(-1, values.shape[-1]), axis=0))
    return (back, gain_part)

def masked_scores(query, key):
    length = query.shape[0]
    scores = contract_cols(query, key) * query.shape[1] ** (-0.5)
    causal = jnp.arange(length)[:, None] >= jnp.arange(length)[None, :]
    return jnp.where(causal, scores, -1e+30)

def head_forward(items):
    query, key, value = items
    scores = masked_scores(query, key)
    total = jax.nn.logsumexp(scores, axis=-1)
    probs = jnp.exp(scores - total[:, None]).astype(jnp.bfloat16)
    mixed = jnp.dot(probs, value, preferred_element_type=jnp.float32).astype(jnp.bfloat16)
    return (mixed, total)

def head_backward(items):
    query, key, value, total, grad_mixed = items
    scores = masked_scores(query, key)
    probs = jnp.exp(scores - total[:, None])
    grad_value = contract_rows(probs.astype(jnp.bfloat16), grad_mixed)
    grad_probs = contract_cols(grad_mixed, value)
    inner = lax.optimization_barrier(jnp.sum(probs * grad_probs, axis=-1, keepdims=True))
    grad_scores = (probs * (grad_probs - inner) * query.shape[1] ** (-0.5)).astype(jnp.bfloat16)
    grad_query = jnp.dot(grad_scores, key, preferred_element_type=jnp.float32)
    grad_key = contract_rows(grad_scores, query)
    return (grad_query, grad_key, grad_value)

def reference(layer_in, w_query, w_key, w_value, w_output, w_gate_up, w_down, pre_gain, mid_gain, query_gain, key_gain, out_grad):
    count = layer_in.shape[0] // L
    group = HQ // KV
    cosine, sine = rope_tables(jnp.arange(L), HD)
    gate_up_flat = w_gate_up.reshape(D, 2 * FF)

    def one_sequence(carry, pair):
        inputs, cotangent = pair
        inputs_wide = inputs.astype(jnp.float32)
        normed_pre, scale_pre = rms_forward(inputs_wide, pre_gain)
        normed_pre = normed_pre.astype(jnp.bfloat16)
        query = jnp.dot(normed_pre, w_query, preferred_element_type=jnp.float32).reshape(L, HQ, HD)
        keys = jnp.dot(normed_pre, w_key, preferred_element_type=jnp.float32).reshape(L, KV, HD)
        values = jnp.dot(normed_pre, w_value, preferred_element_type=jnp.float32).astype(jnp.bfloat16).reshape(L, KV, HD)
        query_normed, query_scale = rms_forward(query, query_gain)
        keys_normed, keys_scale = rms_forward(keys, key_gain)
        query_rot = rotate(query_normed, cosine, sine).astype(jnp.bfloat16)
        keys_rot = rotate(keys_normed, cosine, sine).astype(jnp.bfloat16)
        query_items = query_rot.transpose(1, 0, 2)
        keys_items = jnp.repeat(keys_rot, group, axis=1).transpose(1, 0, 2)
        value_items = jnp.repeat(values, group, axis=1).transpose(1, 0, 2)
        mixed, totals = lax.map(head_forward, (query_items, keys_items, value_items))
        attention = mixed.transpose(1, 0, 2).reshape(L, HQ * HD)
        resid = inputs_wide + jnp.dot(attention, w_output, preferred_element_type=jnp.float32)
        normed_mid, scale_mid = rms_forward(resid, mid_gain)
        normed_mid = normed_mid.astype(jnp.bfloat16)
        gate_up = jnp.dot(normed_mid, gate_up_flat, preferred_element_type=jnp.float32).reshape(L, 2, FF)
        gate = gate_up[:, 0]
        upper = gate_up[:, 1]
        sigma = jax.nn.sigmoid(gate)
        silu = gate * sigma
        hidden = (silu * upper).astype(jnp.bfloat16)
        result = (resid + jnp.dot(hidden, w_down, preferred_element_type=jnp.float32)).astype(jnp.bfloat16)
        grad_hidden = contract_cols(cotangent, w_down)
        part_down = contract_rows(hidden, cotangent)
        grad_gate = grad_hidden * upper * sigma * (1.0 + gate * (1.0 - sigma))
        grad_up = grad_hidden * silu
        grad_flat = jnp.stack([grad_gate, grad_up], axis=1).astype(jnp.bfloat16).reshape(L, 2 * FF)
        part_gate_up = contract_rows(normed_mid, grad_flat).reshape(D, 2, FF)
        grad_mid_in = contract_cols(grad_flat, gate_up_flat)
        back_mid, part_mid = rms_back(resid, scale_mid, mid_gain, grad_mid_in)
        grad_resid = cotangent.astype(jnp.float32) + back_mid
        grad_resid_b = grad_resid.astype(jnp.bfloat16)
        part_output = contract_rows(attention, grad_resid_b)
        grad_attn = contract_cols(grad_resid_b, w_output).astype(jnp.bfloat16)
        grad_items = grad_attn.reshape(L, HQ, HD).transpose(1, 0, 2)
        grad_q, grad_k, grad_v = lax.map(head_backward, (query_items, keys_items, value_items, totals, grad_items))
        grad_q = grad_q.transpose(1, 0, 2)
        grad_k = grad_k.transpose(1, 0, 2).reshape(L, KV, group, HD).sum(axis=2)
        grad_v = grad_v.transpose(1, 0, 2).reshape(L, KV, group, HD).sum(axis=2)
        back_query, part_qgain = rms_back(query, query_scale, query_gain, unrotate(grad_q, cosine, sine))
        back_keys, part_kgain = rms_back(keys, keys_scale, key_gain, unrotate(grad_k, cosine, sine))
        query_b = back_query.reshape(L, HQ * HD).astype(jnp.bfloat16)
        keys_b = back_keys.reshape(L, KV * HD).astype(jnp.bfloat16)
        values_b = grad_v.reshape(L, KV * HD).astype(jnp.bfloat16)
        part_query = contract_rows(normed_pre, query_b)
        part_key = contract_rows(normed_pre, keys_b)
        part_value = contract_rows(normed_pre, values_b)
        grad_pre_in = contract_cols(query_b, w_query) + contract_cols(keys_b, w_key) + contract_cols(values_b, w_value)
        back_pre, part_pre = rms_back(inputs_wide, scale_pre, pre_gain, grad_pre_in)
        grad_input = (grad_resid + back_pre).astype(jnp.bfloat16)
        parts = (part_query, part_key, part_value, part_output, part_gate_up, part_down, part_pre, part_mid, part_qgain, part_kgain)
        carry = tuple((old + new for old, new in zip(carry, parts)))
        return (carry, (result, grad_input))
    zeros = (jnp.zeros((D, HQ * HD), jnp.float32), jnp.zeros((D, KV * HD), jnp.float32), jnp.zeros((D, KV * HD), jnp.float32), jnp.zeros((HQ * HD, D), jnp.float32), jnp.zeros((D, 2, FF), jnp.float32), jnp.zeros((FF, D), jnp.float32), jnp.zeros((D,), jnp.float32), jnp.zeros((D,), jnp.float32), jnp.zeros((HD,), jnp.float32), jnp.zeros((HD,), jnp.float32))
    sums, (results, grad_inputs) = lax.scan(one_sequence, zeros, (layer_in.reshape(count, L, D), out_grad.reshape(count, L, D)))
    return (results.reshape(count * L, D), grad_inputs.reshape(count * L, D), sums[0], sums[1], sums[2], sums[3], sums[4], sums[5], sums[6], sums[7], sums[8], sums[9])
```

```python
import functools

import jax
import jax.numpy as jnp
from jax import lax
from jax.experimental import pallas as pl
from jax.experimental.pallas import tpu as pltpu
from jax.sharding import PartitionSpec as P

L = 1024


EPS = 1e-06
THETA = 1000000.0
F32 = jnp.float32
BF16 = jnp.bfloat16
BLOCK = 256


barrier = lax.optimization_barrier


def dot(left, right):
    return jnp.dot(left, right, preferred_element_type=F32)


def contract_rows(left, right):
    return lax.dot_general(left, right, (((0,), (0,)), ((), ())), preferred_element_type=F32)


def contract_cols(left, right):
    return lax.dot_general(left, right, (((1,), (1,)), ((), ())), preferred_element_type=F32)


def rope_tables(head_size):
    half = head_size // 2
    freq = THETA ** (-(jnp.arange(half, dtype=F32) * 2.0) / head_size)
    angle = jnp.arange(L).astype(F32)[:, None] * freq[None, :]
    cosine, sine = jnp.cos(angle), jnp.sin(angle)
    return (
        jnp.concatenate([cosine, cosine], axis=1),
        jnp.concatenate([-sine, sine], axis=1),
    )


def rms_scale(values):
    return lax.rsqrt(jnp.mean(values * values, axis=-1, keepdims=True) + EPS)


def rms_back(normal, scale, gain, grads):
    scaled = grads * gain
    inner = jnp.mean(scaled * normal, axis=-1, keepdims=True)
    return scale * (scaled - normal * inner)


def turn(values):
    return pltpu.roll(values, values.shape[-1] // 2, 1)


def causal_block(scores_t):
    keys = lax.broadcasted_iota(jnp.int32, scores_t.shape, 0)
    queries = lax.broadcasted_iota(jnp.int32, scores_t.shape, 1)
    return keys <= queries


def attention_forward(group, size, q_ref, k_ref, v_ref, cos_ref, sin_ref, gq_ref, gk_ref, out_ref, lse_ref):
    cosine, sine = cos_ref[...], sin_ref[...]
    factor = size ** (-0.5)
    keys = k_ref[...]
    keys = keys * rms_scale(keys) * gk_ref[...]
    keys = (keys * cosine + turn(keys) * sine).astype(BF16)
    values_t = v_ref[...].T.astype(BF16)
    for h in range(group):
        query = q_ref[:, h * size : (h + 1) * size]
        query = query * rms_scale(query) * gq_ref[...]
        query = (query * cosine + turn(query) * sine).astype(BF16)
        for b in range(L // BLOCK):
            lo, hi = b * BLOCK, (b + 1) * BLOCK
            scores = contract_cols(keys[:hi], query[lo:hi]) * factor
            powers = jnp.exp(scores)
            last = jnp.where(causal_block(powers[lo:]), powers[lo:], 0.0)
            powers = jnp.concatenate([powers[:lo], last], axis=0) if lo else last
            total = jnp.sum(powers, axis=0, keepdims=True)
            probs = (powers * (1.0 / total)).astype(BF16)
            mixed_t = dot(values_t[:, :hi], probs)
            out_ref[lo:hi, h * size : (h + 1) * size] = mixed_t.T.astype(BF16)
            lse_ref[0, h : h + 1, lo:hi] = jnp.log(total)


def attention_backward(
    group, size, heads, kv_heads, q_ref, k_ref, v_ref, grad_ref, lse_ref, cos_ref, sin_ref, gq_ref, gk_ref,
    out_ref, gain_ref, dk_ref, dv_ref, dq_ref,
):
    first = (pl.program_id(0) == 0) & (pl.program_id(1) == 0)

    @pl.when(first)
    def _():
        gain_ref[...] = jnp.zeros_like(gain_ref)

    at = pl.program_id(1)
    cosine, sine = cos_ref[...], sin_ref[...]
    factor = size ** (-0.5)
    raw_k = k_ref[...]
    scale_k = rms_scale(raw_k)
    normal_k = raw_k * scale_k
    keys = normal_k * gk_ref[...]
    keys = keys * cosine + turn(keys) * sine
    keys_t = keys.T.astype(BF16)
    keys = keys.astype(BF16)
    values = v_ref[...].astype(BF16)
    dk_ref[...] = jnp.zeros_like(dk_ref)
    dv_ref[...] = jnp.zeros_like(dv_ref)
    for h in range(group):
        cols = slice(h * size, (h + 1) * size)
        raw_q = q_ref[:, cols]
        scale_q = rms_scale(raw_q)
        normal_q = raw_q * scale_q
        query = normal_q * gq_ref[...]
        query = (query * cosine + turn(query) * sine).astype(BF16)
        grad = grad_ref[:, cols]
        for b in range(L // BLOCK):
            lo, hi = b * BLOCK, (b + 1) * BLOCK
            q_b, g_b = query[lo:hi], grad[lo:hi]
            scores = contract_cols(keys[:hi], q_b) * factor
            probs = jnp.exp(scores - lse_ref[0, h : h + 1, lo:hi])
            last = jnp.where(causal_block(probs[lo:]), probs[lo:], 0.0)
            probs = jnp.concatenate([probs[:lo], last], axis=0) if lo else last
            dv_ref[:hi] += dot(probs.astype(BF16), g_b)
            grad_probs = contract_cols(values[:hi], g_b)
            inner = jnp.sum(probs * grad_probs, axis=0, keepdims=True)
            grad_scores = (probs * (grad_probs - inner) * factor).astype(BF16)
            dk_ref[:hi] += dot(grad_scores, q_b)
            dq_ref[lo:hi] = dot(keys_t[:, :hi], grad_scores).T
        dq = dq_ref[...]
        dqn = dq * cosine - turn(dq) * sine
        gain_ref[0:1] += jnp.sum(dqn * normal_q, axis=0, keepdims=True)
        back = rms_back(normal_q, scale_q, gq_ref[...], dqn)
        out_ref[:, pl.ds(pl.multiple_of((at * group + h) * size, size), size)] = back.astype(BF16)
    dk = dk_ref[...]
    dkn = dk * cosine - turn(dk) * sine
    gain_ref[1:2] += jnp.sum(dkn * normal_k, axis=0, keepdims=True)
    back = rms_back(normal_k, scale_k, gk_ref[...], dkn)
    out_ref[:, pl.ds(pl.multiple_of((heads + at) * size, size), size)] = back.astype(BF16)
    out_ref[:, pl.ds(pl.multiple_of((heads + kv_heads + at) * size, size), size)] = dv_ref[...].astype(BF16)


def hidden_kernel(
    mid_ref, og_ref, gate_ref, up_ref, down_ref, hidden_ref, grad_gate_ref, grad_up_ref, back_ref, out_ref
):
    mid, gate_w, up_w, down_w = mid_ref[...], gate_ref[0], up_ref[0], down_ref[...]
    gate = dot(mid, gate_w)
    upper = dot(mid, up_w)
    grad_hidden = contract_cols(og_ref[...], down_w)
    sigma = 1.0 / (1.0 + jnp.exp(-gate))
    silu = gate * sigma
    hidden = (silu * upper).astype(BF16)
    grad_gate = (grad_hidden * upper * sigma * (1.0 + gate * (1.0 - sigma))).astype(BF16)
    grad_up = (grad_hidden * silu).astype(BF16)
    hidden_ref[...] = hidden
    grad_gate_ref[...] = grad_gate
    grad_up_ref[...] = grad_up
    back = contract_cols(grad_gate, gate_w) + contract_cols(grad_up, up_w)
    out = dot(hidden, down_w)

    @pl.when(pl.program_id(0) == 0)
    def _():
        back_ref[...] = back
        out_ref[...] = out

    @pl.when(pl.program_id(0) > 0)
    def _():
        back_ref[...] += back
        out_ref[...] += out


def hidden_piece(mid, og, gate_up_w, down_w):
    rows, width = mid.shape
    units = down_w.shape[0]
    tile = min(512, units)
    whole = pl.BlockSpec((rows, width), lambda j: (0, 0))
    out = pl.BlockSpec((rows, tile), lambda j: (0, j))
    return pl.pallas_call(
        hidden_kernel,
        grid=(units // tile,),
        in_specs=[
            whole,
            whole,
            pl.BlockSpec((1, width, tile), lambda j: (0, 0, j)),
            pl.BlockSpec((1, width, tile), lambda j: (1, 0, j)),
            pl.BlockSpec((tile, width), lambda j: (j, 0)),
        ],
        out_specs=(out, out, out, whole, whole),
        out_shape=tuple(jax.ShapeDtypeStruct((rows, units), BF16) for _ in range(3))
        + tuple(jax.ShapeDtypeStruct((rows, width), F32) for _ in range(2)),
        cost_estimate=pl.CostEstimate(
            flops=12 * rows * width * units,
            transcendentals=rows * units,
            bytes_accessed=6 * width * units + 12 * rows * width + 6 * rows * units,
        ),
        name="hidden_piece",
    )(mid, og, gate_up_w, gate_up_w, down_w)


def qkv_specs(group, size, heads, kv_heads):
    return [
        pl.BlockSpec((L, group * size), lambda s, g: (s, g)),
        pl.BlockSpec((L, size), lambda s, g: (s, heads + g)),
        pl.BlockSpec((L, size), lambda s, g: (s, heads + kv_heads + g)),
    ]


def forward_heads(qkv, cosine, sine, gain_q, gain_k, heads, kv_heads):
    rows, size, group = qkv.shape[0], cosine.shape[1], heads // kv_heads
    fixed = pl.BlockSpec((L, size), lambda s, g: (0, 0))
    gain = pl.BlockSpec((1, size), lambda s, g: (0, 0))
    return pl.pallas_call(
        functools.partial(attention_forward, group, size),
        grid=(rows // L, kv_heads),
        in_specs=qkv_specs(group, size, heads, kv_heads) + [fixed, fixed, gain, gain],
        out_specs=(
            pl.BlockSpec((L, group * size), lambda s, g: (s, g)),
            pl.BlockSpec((1, group, L), lambda s, g: (s * kv_heads + g, 0, 0)),
        ),
        out_shape=(
            jax.ShapeDtypeStruct((rows, heads * size), BF16),
            jax.ShapeDtypeStruct((rows // L * kv_heads, group, L), F32),
        ),
        cost_estimate=pl.CostEstimate(
            flops=4 * heads * rows * L * size,
            transcendentals=heads * rows * L,
            bytes_accessed=rows * (heads + 2 * kv_heads) * size * 4 + rows * heads * size * 2,
        ),
        name="attention_forward",
    )(qkv, qkv, qkv, cosine, sine, gain_q, gain_k)


def backward_heads(qkv, grad, lse, cosine, sine, gain_q, gain_k, heads, kv_heads):
    rows, size, group = qkv.shape[0], cosine.shape[1], heads // kv_heads
    width = (heads + 2 * kv_heads) * size
    fixed = pl.BlockSpec((L, size), lambda s, g: (0, 0))
    gain = pl.BlockSpec((1, size), lambda s, g: (0, 0))
    return pl.pallas_call(
        functools.partial(attention_backward, group, size, heads, kv_heads),
        grid=(rows // L, kv_heads),
        in_specs=qkv_specs(group, size, heads, kv_heads)
        + [
            pl.BlockSpec((L, group * size), lambda s, g: (s, g)),
            pl.BlockSpec((1, group, L), lambda s, g: (s * kv_heads + g, 0, 0)),
            fixed,
            fixed,
            gain,
            gain,
        ],
        out_specs=(
            pl.BlockSpec((L, width), lambda s, g: (s, 0)),
            pl.BlockSpec((2, size), lambda s, g: (0, 0)),
        ),
        out_shape=(
            jax.ShapeDtypeStruct((rows, width), BF16),
            jax.ShapeDtypeStruct((2, size), F32),
        ),
        scratch_shapes=[pltpu.VMEM((L, size), F32)] * 3,
        cost_estimate=pl.CostEstimate(
            flops=10 * heads * rows * L * size,
            transcendentals=heads * rows * L,
            bytes_accessed=rows * width * 6 + rows * heads * size * 2,
        ),
        name="attention_backward",
    )(qkv, qkv, qkv, grad, lse, cosine, sine, gain_q, gain_k)


def on_device(
    devices,
    layer_in,
    w_query,
    w_key,
    w_value,
    w_output,
    w_gate_up,
    w_down,
    pre_gain,
    mid_gain,
    query_gain,
    key_gain,
    out_grad,
):
    dp, parts = devices
    ring = [(i, (i + 1) % parts) for i in range(parts)]
    me = lax.axis_index("tensor")
    mine = lax.axis_index("dp")
    rows, width = layer_in.shape
    all_rows = rows * parts
    head_size = query_gain.shape[0] * dp
    heads = w_query.shape[1] // head_size
    kv_heads = w_key.shape[1] // head_size

    def place(k):
        return (me + parts - k) % parts

    def around(block):
        return lax.ppermute(block, "tensor", ring)

    def gather_ring(block):
        blocks = [block]
        for _ in range(parts - 1):
            blocks.append(around(blocks[-1]))
        return blocks

    def scatter_ring(part, fillers=()):
        order = list(range(1, parts)) + [0]
        made = []
        total = part(order[0])
        for j, k in enumerate(order[1:]):
            moving = around(total.astype(BF16))
            new = fillers[j]() if j < len(fillers) else ()
            moving, ahead, new = barrier((moving, part(k), new))
            total = ahead + moving.astype(F32)
            made.append(new)
        return total, made

    def scattered(part, axis):
        return lax.psum_scatter(part, "dp", scatter_dimension=axis, tiled=True)

    bits = dp.bit_length() - 1

    def halve(block, left, bit):
        axis, own = left.index(bit), (mine >> bit) & 1
        keep, give = (lax.dynamic_index_in_dim(block, at, axis, keepdims=False) for at in (own, 1 - own))
        took = lax.ppermute(give, "dp", [(i, i ^ (1 << bit)) for i in range(dp)])
        return (keep.astype(F32) + took.astype(F32)).astype(BF16), [b for b in left if b != bit]

    def halves_start(part):
        block = part.reshape((2,) * bits + (part.shape[0] // dp, part.shape[1]))
        return halve(block, list(range(bits))[::-1], 0)

    def halves_split(state):
        block, left = state
        cut = block.shape[-1] // 2
        rest = sorted(left)
        return [(block[..., :cut], left, rest), (block[..., cut:], left, rest[::-1])]

    def halves_step(states):
        return [(*halve(block, left, order[0]), order[1:]) for block, left, order in states]

    def halves_end(states):
        while states[0][2]:
            states = halves_step(states)
        return jnp.concatenate([block for block, _, _ in states], axis=-1)

    def butterfly(values):
        for axis, size in (("dp", dp), ("tensor", parts)):
            for bit in range(size.bit_length() - 1):
                values = values + lax.ppermute(values, axis, [(i, i ^ (1 << bit)) for i in range(size)])
        return values

    sizes = (pre_gain.shape[0], mid_gain.shape[0], query_gain.shape[0], key_gain.shape[0])
    used = sum(sizes)
    packed = jnp.concatenate([pre_gain, mid_gain, query_gain, key_gain])
    packed = jnp.pad(packed, (0, -used % 128)).reshape(1, -1)
    output_w = lax.all_gather(w_output, "tensor", axis=0, tiled=True)
    w_qkv = lax.all_gather(jnp.concatenate([w_query, w_key, w_value], axis=1), "dp", axis=0, tiled=True)
    gate_up_w = lax.all_gather(w_gate_up.transpose(1, 0, 2), "dp", axis=1, tiled=True)
    down_w = lax.all_gather(w_down, "dp", axis=1, tiled=True)

    xs = [layer_in, around(layer_in)]
    output_w, packed, _ = barrier((output_w, packed, xs[1]))
    output_w = lax.all_gather(output_w, "dp", axis=1, tiled=True)
    gains = lax.all_gather(packed, "dp", axis=0, tiled=True).astype(F32)
    starts = [sum(sizes[:i]) for i in range(5)]
    pre_full, mid_full, gain_query, gain_key = (
        gains[:, lo:hi].reshape(1, -1) for lo, hi in zip(starts, starts[1:])
    )
    cosine, sine = rope_tables(head_size)

    normals = []
    qkv = jnp.zeros((all_rows, w_qkv.shape[1]), F32)
    normed_full = jnp.zeros((all_rows, width), BF16)
    for k in range(parts):
        if 0 < k < parts - 1:
            xs.append(around(xs[k]))
        wide = xs[k].astype(F32)
        scale = rms_scale(wide)
        normals.append((wide, scale))
        normed = (wide * scale * pre_full).astype(BF16)
        at = (place(k) * rows, 0)
        normed_full = lax.dynamic_update_slice(normed_full, normed, at)
        qkv = lax.dynamic_update_slice(qkv, dot(normed, w_qkv), at)
        if k == parts - 2:
            qkv, normed_full, xs[-1] = barrier((qkv, normed_full, xs[-1]))

    first_og, _ = barrier((out_grad, xs[-1]))
    ogs = [out_grad, around(first_og)]
    attention, lse = forward_heads(qkv, cosine, sine, gain_query, gain_key, heads, kv_heads)
    attention, ogs[1] = barrier((attention, ogs[1]))
    ogs.append(around(ogs[1]))
    mixed = lax.all_to_all(
        attention.reshape(parts, rows, heads * head_size), "tensor", 0, 0, tiled=True
    )
    mixed = mixed.transpose(1, 0, 2).reshape(rows, parts * heads * head_size)
    mixed, ogs[-1] = barrier((mixed, ogs[-1]))
    for k in range(2, parts - 1):
        ogs.append(around(ogs[k]))
    inputs_wide = normals[0][0]
    resid = inputs_wide + dot(mixed, output_w)
    scale_mid = rms_scale(resid)
    normal_mid = resid * scale_mid
    mids = gather_ring((normal_mid * mid_full).astype(BF16))

    pieces = {}

    def back_part(k):
        pieces[k] = hidden_piece(mids[k], ogs[k], gate_up_w, down_w)
        return pieces[k][3]

    def rows_of(blocks):
        return jnp.concatenate(blocks, axis=0)

    def column(i):
        return [pieces[k][i] for k in range(parts)]

    def all_pieces():
        for k in range(2, parts):
            back_part(k)
        back_part(0)
        return ()

    back_part(1)
    grad_mid_in, (_, part_gate, (part_up, part_down)) = scatter_ring(
        lambda k: pieces[k][3],
        (
            all_pieces,
            lambda: contract_rows(rows_of(mids), rows_of(column(1))).astype(BF16),
            lambda: (
                contract_rows(rows_of(mids), rows_of(column(2))).astype(BF16),
                contract_rows(rows_of(column(0)), rows_of(ogs)).astype(BF16),
            ),
        ),
    )
    summed_gate, summed_down = scattered(part_gate, 0), scattered(part_down, 1)
    grad_resid = out_grad.astype(F32) + rms_back(normal_mid, scale_mid, mid_full, grad_mid_in)
    part_mid = jnp.sum(grad_mid_in * normal_mid, axis=0)
    grad_resid_b = grad_resid.astype(BF16)

    late = barrier((column(4), grad_resid_b))[0]
    down_move = around(late[1].astype(BF16))
    grad_mixed = contract_cols(grad_resid_b, output_w).astype(BF16)
    grad_mixed = grad_mixed.reshape(rows, parts, heads * head_size).transpose(1, 0, 2)
    grad_attn = lax.all_to_all(grad_mixed, "tensor", 0, 0, tiled=True).reshape(all_rows, heads * head_size)
    up_state = halves_step(halves_split(halves_start(part_up)))
    part_output = contract_rows(grad_resid_b, mixed).astype(BF16)
    grad_attn, down_move, part_output, up_blocks = barrier(
        (grad_attn, down_move, part_output, [u[0] for u in up_state])
    )
    up_state = [(block, *u[1:]) for block, u in zip(up_blocks, up_state)]
    down_move = around((late[2] + down_move.astype(F32)).astype(BF16))
    out_block, out_left = halves_start(part_output)

    grad_qkv, gain_parts = backward_heads(
        qkv, grad_attn, lse, cosine, sine, gain_query, gain_key, heads, kv_heads
    )
    grad_qkv, down_move, out_block, summed_up, summed_gate = barrier(
        (grad_qkv, down_move, out_block, halves_end(up_state), summed_gate)
    )
    for k in range(3, parts):
        down_move = around((late[k] + down_move.astype(F32)).astype(BF16))
    layer_out = (resid + late[0] + down_move.astype(F32)).astype(BF16)

    grads_in, part_pre = [], 0.0
    for k in range(parts):
        block = lax.dynamic_slice(grad_qkv, (place(k) * rows, 0), (rows, grad_qkv.shape[1]))
        grads_in.append(contract_cols(block, w_qkv))
        wide, scale = normals[k]
        part_pre = part_pre + jnp.sum(grads_in[k] * (wide * scale), axis=0)

    def gain_filler():
        packed = jnp.concatenate([part_pre, part_mid, gain_parts[0], gain_parts[1]])
        return butterfly(packed.reshape(-1, 128)).reshape(-1), summed_down

    grad_pre_in, ((part_qkv, out_rows), (gain_sums, summed_down), _) = scatter_ring(
        lambda k: grads_in[k],
        (
            lambda: (
                contract_rows(normed_full, grad_qkv).astype(BF16),
                halves_end(halves_split((out_block, out_left))),
            ),
            gain_filler,
        ),
    )
    summed_qkv = scattered(part_qkv, 0).astype(F32)
    out_cols = out_rows.shape[1] // parts
    summed_output, _ = scatter_ring(
        lambda k: lax.dynamic_slice(
            out_rows, (0, place(k) * out_cols), (out_rows.shape[0], out_cols)
        ).astype(F32)
    )
    summed_output = summed_output.T
    scale_pre = normals[0][1]
    back_pre = rms_back(inputs_wide * scale_pre, scale_pre, pre_full, grad_pre_in)
    in_grad = (grad_resid + back_pre).astype(BF16)

    summed_down = summed_down.astype(F32)
    summed_gate_up = jnp.stack([summed_gate.astype(F32), summed_up.astype(F32)], axis=1)
    cuts = [w_query.shape[1], w_query.shape[1] + w_key.shape[1]]
    summed_query, summed_key, summed_value = jnp.split(summed_qkv, cuts, axis=1)

    outs, at = [], 0
    for full, size in zip((width, width, head_size, head_size), sizes):
        outs.append(lax.dynamic_slice(gain_sums, (at + mine * size,), (size,)))
        at += full
    return (
        layer_out,
        in_grad,
        summed_query,
        summed_key,
        summed_value,
        summed_output,
        summed_gate_up,
        summed_down,
        *outs,
    )


def solution(mesh):
    placed = (
        P(("dp", "tensor"), None),
        P("dp", "tensor"),
        P("dp", "tensor"),
        P("dp", "tensor"),
        P("tensor", "dp"),
        P("dp", None, "tensor"),
        P("tensor", "dp"),
        P("dp"),
        P("dp"),
        P("dp"),
        P("dp"),
        P(("dp", "tensor"), None),
    )
    return jax.shard_map(
        functools.partial(on_device, (mesh.shape["dp"], mesh.shape["tensor"])),
        mesh=mesh,
        in_specs=placed,
        out_specs=(
            P(("dp", "tensor"), None),
            P(("dp", "tensor"), None),
            P("dp", "tensor"),
            P("dp", "tensor"),
            P("dp", "tensor"),
            P("tensor", "dp"),
            P("dp", None, "tensor"),
            P("tensor", "dp"),
            P("dp"),
            P("dp"),
            P("dp"),
            P("dp"),
        ),
        check_vma=False,
    )
```

```python
import functools

import jax
import jax.numpy as jnp
from jax import lax
from jax.experimental import pallas as pl
from jax.experimental.pallas import tpu as pltpu
from jax.sharding import PartitionSpec as P

L = 1024


EPS = 1e-06
THETA = 1000000.0
F32 = jnp.float32
BF16 = jnp.bfloat16
BLOCK = 256


barrier = lax.optimization_barrier


def dot(left, right):
    return jnp.dot(left, right, preferred_element_type=F32)


def contract_rows(left, right):
    return lax.dot_general(left, right, (((0,), (0,)), ((), ())), preferred_element_type=F32)


def contract_cols(left, right):
    return lax.dot_general(left, right, (((1,), (1,)), ((), ())), preferred_element_type=F32)


def rope_tables(head_size):
    half = head_size // 2
    freq = THETA ** (-(jnp.arange(half, dtype=F32) * 2.0) / head_size)
    angle = jnp.arange(L).astype(F32)[:, None] * freq[None, :]
    cosine, sine = jnp.cos(angle), jnp.sin(angle)
    return (
        jnp.concatenate([cosine, cosine], axis=1),
        jnp.concatenate([-sine, sine], axis=1),
    )


def rms_scale(values):
    return lax.rsqrt(jnp.mean(values * values, axis=-1, keepdims=True) + EPS)


def rms_back(normal, scale, gain, grads):
    scaled = grads * gain
    inner = jnp.mean(scaled * normal, axis=-1, keepdims=True)
    return scale * (scaled - normal * inner)


def turn(values):
    return pltpu.roll(values, values.shape[-1] // 2, 1)


def causal_block(scores_t):
    keys = lax.broadcasted_iota(jnp.int32, scores_t.shape, 0)
    queries = lax.broadcasted_iota(jnp.int32, scores_t.shape, 1)
    return keys <= queries


def attention_forward(group, size, q_ref, k_ref, v_ref, cos_ref, sin_ref, gq_ref, gk_ref, out_ref, lse_ref):
    cosine, sine = cos_ref[...], sin_ref[...]
    factor = size ** (-0.5)
    keys = k_ref[...]
    keys = keys * rms_scale(keys) * gk_ref[...]
    keys = (keys * cosine + turn(keys) * sine).astype(BF16)
    values_t = v_ref[...].T.astype(BF16)
    for h in range(group):
        query = q_ref[:, h * size : (h + 1) * size]
        query = query * rms_scale(query) * gq_ref[...]
        query = (query * cosine + turn(query) * sine).astype(BF16)
        for b in range(L // BLOCK):
            lo, hi = b * BLOCK, (b + 1) * BLOCK
            scores = contract_cols(keys[:hi], query[lo:hi]) * factor
            powers = jnp.exp(scores)
            last = jnp.where(causal_block(powers[lo:]), powers[lo:], 0.0)
            powers = jnp.concatenate([powers[:lo], last], axis=0) if lo else last
            total = jnp.sum(powers, axis=0, keepdims=True)
            probs = (powers * (1.0 / total)).astype(BF16)
            mixed_t = dot(values_t[:, :hi], probs)
            out_ref[lo:hi, h * size : (h + 1) * size] = mixed_t.T.astype(BF16)
            lse_ref[0, h : h + 1, lo:hi] = jnp.log(total)


def attention_backward(
    group, size, heads, kv_heads, q_ref, k_ref, v_ref, grad_ref, lse_ref, cos_ref, sin_ref, gq_ref, gk_ref,
    out_ref, gain_ref, dk_ref, dv_ref, dq_ref,
):
    first = (pl.program_id(0) == 0) & (pl.program_id(1) == 0)

    @pl.when(first)
    def _():
        gain_ref[...] = jnp.zeros_like(gain_ref)

    at = pl.program_id(1)
    cosine, sine = cos_ref[...], sin_ref[...]
    factor = size ** (-0.5)
    raw_k = k_ref[...]
    scale_k = rms_scale(raw_k)
    normal_k = raw_k * scale_k
    keys = normal_k * gk_ref[...]
    keys = keys * cosine + turn(keys) * sine
    keys_t = keys.T.astype(BF16)
    keys = keys.astype(BF16)
    values = v_ref[...].astype(BF16)
    dk_ref[...] = jnp.zeros_like(dk_ref)
    dv_ref[...] = jnp.zeros_like(dv_ref)
    for h in range(group):
        cols = slice(h * size, (h + 1) * size)
        raw_q = q_ref[:, cols]
        scale_q = rms_scale(raw_q)
        normal_q = raw_q * scale_q
        query = normal_q * gq_ref[...]
        query = (query * cosine + turn(query) * sine).astype(BF16)
        grad = grad_ref[:, cols]
        for b in range(L // BLOCK):
            lo, hi = b * BLOCK, (b + 1) * BLOCK
            q_b, g_b = query[lo:hi], grad[lo:hi]
            scores = contract_cols(keys[:hi], q_b) * factor
            probs = jnp.exp(scores - lse_ref[0, h : h + 1, lo:hi])
            last = jnp.where(causal_block(probs[lo:]), probs[lo:], 0.0)
            probs = jnp.concatenate([probs[:lo], last], axis=0) if lo else last
            dv_ref[:hi] += dot(probs.astype(BF16), g_b)
            grad_probs = contract_cols(values[:hi], g_b)
            inner = jnp.sum(probs * grad_probs, axis=0, keepdims=True)
            grad_scores = (probs * (grad_probs - inner) * factor).astype(BF16)
            dk_ref[:hi] += dot(grad_scores, q_b)
            dq_ref[lo:hi] = dot(keys_t[:, :hi], grad_scores).T
        dq = dq_ref[...]
        dqn = dq * cosine - turn(dq) * sine
        gain_ref[0:1] += jnp.sum(dqn * normal_q, axis=0, keepdims=True)
        back = rms_back(normal_q, scale_q, gq_ref[...], dqn)
        out_ref[:, pl.ds(pl.multiple_of((at * group + h) * size, size), size)] = back.astype(BF16)
    dk = dk_ref[...]
    dkn = dk * cosine - turn(dk) * sine
    gain_ref[1:2] += jnp.sum(dkn * normal_k, axis=0, keepdims=True)
    back = rms_back(normal_k, scale_k, gk_ref[...], dkn)
    out_ref[:, pl.ds(pl.multiple_of((heads + at) * size, size), size)] = back.astype(BF16)
    out_ref[:, pl.ds(pl.multiple_of((heads + kv_heads + at) * size, size), size)] = dv_ref[...].astype(BF16)


def hidden_kernel(blocks, *refs):
    gate_refs, up_refs = refs[:blocks], refs[blocks : 2 * blocks]
    mid_ref, og_ref, down_ref, hidden_ref, grad_gate_ref, grad_up_ref, back_ref, out_ref = refs[2 * blocks :]
    gate_w = jnp.concatenate([ref[...] for ref in gate_refs], axis=0)
    up_w = jnp.concatenate([ref[...] for ref in up_refs], axis=0)
    mid, down_w = mid_ref[...], down_ref[...]
    gate = dot(mid, gate_w)
    upper = dot(mid, up_w)
    grad_hidden = contract_cols(og_ref[...], down_w)
    sigma = 1.0 / (1.0 + jnp.exp(-gate))
    silu = gate * sigma
    hidden = (silu * upper).astype(BF16)
    grad_gate = (grad_hidden * upper * sigma * (1.0 + gate * (1.0 - sigma))).astype(BF16)
    grad_up = (grad_hidden * silu).astype(BF16)
    hidden_ref[...] = hidden
    grad_gate_ref[...] = grad_gate
    grad_up_ref[...] = grad_up
    back = contract_cols(grad_gate, gate_w) + contract_cols(grad_up, up_w)
    out = dot(hidden, down_w)

    @pl.when(pl.program_id(0) == 0)
    def _():
        back_ref[...] = back
        out_ref[...] = out

    @pl.when(pl.program_id(0) > 0)
    def _():
        back_ref[...] += back
        out_ref[...] += out


def hidden_piece(mid, og, gate_blocks, up_blocks, down_w):
    rows, width = mid.shape
    units = down_w.shape[0]
    blocks = len(gate_blocks)
    tile = min(512, units)
    whole = pl.BlockSpec((rows, width), lambda j: (0, 0))
    out = pl.BlockSpec((rows, tile), lambda j: (0, j))
    block = pl.BlockSpec((width // blocks, tile), lambda j: (0, j))
    return pl.pallas_call(
        functools.partial(hidden_kernel, blocks),
        grid=(units // tile,),
        in_specs=[block] * (2 * blocks) + [whole, whole, pl.BlockSpec((tile, width), lambda j: (j, 0))],
        out_specs=(out, out, out, whole, whole),
        out_shape=tuple(jax.ShapeDtypeStruct((rows, units), BF16) for _ in range(3))
        + tuple(jax.ShapeDtypeStruct((rows, width), F32) for _ in range(2)),
        cost_estimate=pl.CostEstimate(
            flops=12 * rows * width * units,
            transcendentals=rows * units,
            bytes_accessed=6 * width * units + 12 * rows * width + 6 * rows * units,
        ),
        name="hidden_piece",
    )(*gate_blocks, *up_blocks, mid, og, down_w)


def shuffle_kernel(size, order_ref, in_ref, out_ref):
    for i in range(in_ref.shape[1] // size):
        at = pl.multiple_of(order_ref[i] * size, size)
        out_ref[:, i * size : (i + 1) * size] = in_ref[:, pl.ds(at, size)]


def shuffled(values, order):
    size = values.shape[1] // order.shape[0]
    if size % 128:
        cut = values.reshape(values.shape[0], order.shape[0], size)
        return cut[:, order].reshape(values.shape)
    whole = pl.BlockSpec(values.shape, lambda i, order: (0, 0))
    return pl.pallas_call(
        functools.partial(shuffle_kernel, size),
        grid_spec=pltpu.PrefetchScalarGridSpec(
            num_scalar_prefetch=1, grid=(1,), in_specs=[whole], out_specs=whole
        ),
        out_shape=jax.ShapeDtypeStruct(values.shape, values.dtype),
        cost_estimate=pl.CostEstimate(
            flops=0, transcendentals=0, bytes_accessed=2 * values.size * values.dtype.itemsize
        ),
        name="shuffled",
    )(order, values)


def qkv_specs(group, size, heads, kv_heads):
    return [
        pl.BlockSpec((L, group * size), lambda s, g: (s, g)),
        pl.BlockSpec((L, size), lambda s, g: (s, heads + g)),
        pl.BlockSpec((L, size), lambda s, g: (s, heads + kv_heads + g)),
    ]


def forward_heads(qkv, cosine, sine, gain_q, gain_k, heads, kv_heads):
    rows, size, group = qkv.shape[0], cosine.shape[1], heads // kv_heads
    fixed = pl.BlockSpec((L, size), lambda s, g: (0, 0))
    gain = pl.BlockSpec((1, size), lambda s, g: (0, 0))
    return pl.pallas_call(
        functools.partial(attention_forward, group, size),
        grid=(rows // L, kv_heads),
        in_specs=qkv_specs(group, size, heads, kv_heads) + [fixed, fixed, gain, gain],
        out_specs=(
            pl.BlockSpec((L, group * size), lambda s, g: (s, g)),
            pl.BlockSpec((1, group, L), lambda s, g: (s * kv_heads + g, 0, 0)),
        ),
        out_shape=(
            jax.ShapeDtypeStruct((rows, heads * size), BF16),
            jax.ShapeDtypeStruct((rows // L * kv_heads, group, L), F32),
        ),
        cost_estimate=pl.CostEstimate(
            flops=4 * heads * rows * L * size,
            transcendentals=heads * rows * L,
            bytes_accessed=rows * (heads + 2 * kv_heads) * size * 4 + rows * heads * size * 2,
        ),
        name="attention_forward",
    )(qkv, qkv, qkv, cosine, sine, gain_q, gain_k)


def backward_heads(qkv, grad, lse, cosine, sine, gain_q, gain_k, heads, kv_heads):
    rows, size, group = qkv.shape[0], cosine.shape[1], heads // kv_heads
    width = (heads + 2 * kv_heads) * size
    fixed = pl.BlockSpec((L, size), lambda s, g: (0, 0))
    gain = pl.BlockSpec((1, size), lambda s, g: (0, 0))
    return pl.pallas_call(
        functools.partial(attention_backward, group, size, heads, kv_heads),
        grid=(rows // L, kv_heads),
        in_specs=qkv_specs(group, size, heads, kv_heads)
        + [
            pl.BlockSpec((L, group * size), lambda s, g: (s, g)),
            pl.BlockSpec((1, group, L), lambda s, g: (s * kv_heads + g, 0, 0)),
            fixed,
            fixed,
            gain,
            gain,
        ],
        out_specs=(
            pl.BlockSpec((L, width), lambda s, g: (s, 0)),
            pl.BlockSpec((2, size), lambda s, g: (0, 0)),
        ),
        out_shape=(
            jax.ShapeDtypeStruct((rows, width), BF16),
            jax.ShapeDtypeStruct((2, size), F32),
        ),
        scratch_shapes=[pltpu.VMEM((L, size), F32)] * 3,
        cost_estimate=pl.CostEstimate(
            flops=10 * heads * rows * L * size,
            transcendentals=heads * rows * L,
            bytes_accessed=rows * width * 6 + rows * heads * size * 2,
        ),
        name="attention_backward",
    )(qkv, qkv, qkv, grad, lse, cosine, sine, gain_q, gain_k)


def on_device(
    devices,
    layer_in,
    w_query,
    w_key,
    w_value,
    w_output,
    w_gate_up,
    w_down,
    pre_gain,
    mid_gain,
    query_gain,
    key_gain,
    out_grad,
):
    dp, parts = devices
    ring = [(i, (i + 1) % parts) for i in range(parts)]
    me = lax.axis_index("tensor")
    mine = lax.axis_index("dp")
    rows, width = layer_in.shape
    all_rows = rows * parts
    head_size = query_gain.shape[0] * dp
    heads = w_query.shape[1] // head_size
    kv_heads = w_key.shape[1] // head_size

    def place(k):
        return (me + parts - k) % parts

    def around(block):
        return lax.ppermute(block, "tensor", ring)

    def gather_ring(block):
        blocks = [block]
        for _ in range(parts - 1):
            blocks.append(around(blocks[-1]))
        return blocks

    def scatter_ring(part, fillers=()):
        order = list(range(1, parts)) + [0]
        made = []
        total = part(order[0])
        for j, k in enumerate(order[1:]):
            moving = around(total.astype(BF16))
            ahead = part(k)
            new = fillers[j]() if j < len(fillers) else ()
            moving, ahead, new = barrier((moving, ahead, new))
            total = ahead + moving.astype(F32)
            made.append(new)
        return total, made

    def scattered(part, axis):
        return lax.psum_scatter(part, "dp", scatter_dimension=axis, tiled=True)

    bits = dp.bit_length() - 1

    def swap(block, bit):
        return lax.ppermute(block, "dp", [(i, i ^ (1 << bit)) for i in range(dp)])

    near_last = list(range(1, bits)) + [0]
    relative = [0]
    for bit in near_last:
        relative = relative + [r | (1 << bit) for r in relative]

    def doubling_step(held, bit):
        return {**held, **{r | (1 << bit): swap(block, bit) for r, block in held.items()}}

    def halving_step(keep, give, bit):
        return (keep.astype(F32) + swap(give, bit).astype(F32)).astype(BF16)

    def halve(held, bit):
        keep = [r for r in held if not (r >> bit) & 1]
        far = swap(jnp.concatenate([held[r | (1 << bit)] for r in keep], axis=0), bit)
        size = far.shape[0] // len(keep)
        return {
            r: (held[r].astype(F32) + far[i * size : (i + 1) * size].astype(F32)).astype(BF16)
            for i, r in enumerate(keep)
        }

    def by_name(block, names):
        size = block.shape[0] // len(names)
        return {r: block[i * size : (i + 1) * size] for i, r in enumerate(names)}

    def butterfly(values):
        for axis, size in (("dp", dp), ("tensor", parts)):
            for bit in range(size.bit_length() - 1):
                values = values + lax.ppermute(values, axis, [(i, i ^ (1 << bit)) for i in range(size)])
        return values

    sizes = (pre_gain.shape[0], mid_gain.shape[0], query_gain.shape[0], key_gain.shape[0])
    used = sum(sizes)
    packed = jnp.concatenate([pre_gain, mid_gain, query_gain, key_gain])
    packed = jnp.pad(packed, (0, -used % 128)).reshape(1, -1)
    w_qkv = lax.all_gather(jnp.concatenate([w_query, w_key, w_value], axis=1), "dp", axis=0, tiled=True)
    xs = [layer_in, around(layer_in)]
    steps = list(zip(near_last, near_last[:-1][::-1] + near_last[-1:]))
    blocks = [{0: w_gate_up[:, 0]}, {0: w_gate_up[:, 1]}]

    def double(hop):
        if steps:
            for i, bit in enumerate(steps.pop(0)):
                blocks[i] = doubling_step(blocks[i], bit)
            blocks[:], hop = barrier((blocks, hop))
        return hop

    xs[1] = double(xs[1])
    w_output, packed, _ = barrier((w_output, packed, xs[1]))
    output_w = lax.all_gather(w_output, "tensor", axis=0, tiled=True)
    gains = lax.all_gather(packed, "dp", axis=0, tiled=True).astype(F32)
    starts = [sum(sizes[:i]) for i in range(5)]
    pre_full, mid_full, gain_query, gain_key = (
        gains[:, lo:hi].reshape(1, -1) for lo, hi in zip(starts, starts[1:])
    )
    cosine, sine = rope_tables(head_size)

    normals = []
    qkv = jnp.zeros((all_rows, w_qkv.shape[1]), F32)
    normed_full = jnp.zeros((all_rows, width), BF16)
    for k in range(parts):
        if 0 < k < parts - 1:
            xs.append(around(xs[k]))
        wide = xs[k].astype(F32)
        scale = rms_scale(wide)
        normals.append((wide, scale))
        normed = (wide * scale * pre_full).astype(BF16)
        at = (place(k) * rows, 0)
        normed_full = lax.dynamic_update_slice(normed_full, normed, at)
        qkv = lax.dynamic_update_slice(qkv, dot(normed, w_qkv), at)
        if k == parts - 2:
            xs[-1] = double(xs[-1])
            qkv, normed_full, xs[-1], output_w = barrier((qkv, normed_full, xs[-1], output_w))
            output_w = lax.all_gather(output_w, "dp", axis=1, tiled=True)

    down_w = lax.all_gather(w_down, "dp", axis=1, tiled=True)
    first_og, _ = barrier((out_grad, xs[-1]))
    ogs = [out_grad, around(first_og)]
    attention, lse = forward_heads(qkv, cosine, sine, gain_query, gain_key, heads, kv_heads)
    ogs[1] = double(ogs[1])
    while steps:
        ogs[1] = double(ogs[1])
    gate_blocks, up_blocks = ([held[r] for r in relative] for held in blocks)
    attention, ogs[1] = barrier((attention, ogs[1]))
    ogs.append(around(ogs[1]))
    mixed = lax.all_to_all(
        attention.reshape(parts, rows, heads * head_size), "tensor", 0, 0, tiled=True
    )
    mixed = mixed.transpose(1, 0, 2).reshape(rows, parts * heads * head_size)
    mixed, ogs[-1] = barrier((mixed, ogs[-1]))
    for k in range(2, parts - 1):
        ogs.append(around(ogs[k]))
    inputs_wide = normals[0][0]
    resid = inputs_wide + dot(mixed, output_w)
    scale_mid = rms_scale(resid)
    normal_mid = resid * scale_mid
    mids = gather_ring(
        shuffled((normal_mid * mid_full).astype(BF16), mine ^ jnp.asarray(relative, jnp.int32))
    )
    pieces = {}

    def piece(k):
        pieces[k] = hidden_piece(mids[k], ogs[k], gate_blocks, up_blocks, down_w)
        return pieces[k][3]

    def rows_of(blocks):
        return jnp.concatenate(blocks, axis=0)

    def column(i):
        return rows_of([pieces[k][i] for k in range(parts)])

    half = width // 2
    piece(1)
    grad_mid_in, made = scatter_ring(
        piece, [tuple] * (parts - 2) + [lambda: contract_rows(column(0), rows_of(ogs)).astype(BF16)]
    )
    part_down = made[-1]
    mid_rows, grad_gates, grad_ups = rows_of(mids), column(1), column(2)
    give_gate, give_up = (contract_rows(mid_rows[:, half:], g).astype(BF16) for g in (grad_gates, grad_ups))
    grad_mid_in, give_gate, give_up = barrier((grad_mid_in, give_gate, give_up))
    summed_down = scattered(part_down, 1)
    back_order = [relative.index(r) for r in range(dp)]
    grad_mid_in = shuffled(
        grad_mid_in, jnp.asarray(back_order, jnp.int32)[mine ^ jnp.arange(dp, dtype=jnp.int32)]
    )
    grad_resid = out_grad.astype(F32) + rms_back(normal_mid, scale_mid, mid_full, grad_mid_in)
    part_mid = jnp.sum(grad_mid_in * normal_mid, axis=0)
    grad_resid_b = grad_resid.astype(BF16)

    late = barrier(([pieces[k][4] for k in range(parts)], grad_resid_b))[0]
    down_move = around(late[1].astype(BF16))
    grad_mixed = contract_cols(grad_resid_b, output_w).astype(BF16)
    grad_mixed = grad_mixed.reshape(rows, parts, heads * head_size).transpose(1, 0, 2)
    grad_attn = lax.all_to_all(grad_mixed, "tensor", 0, 0, tiled=True).reshape(all_rows, heads * head_size)
    part_output = contract_rows(mixed, grad_resid_b).astype(BF16)
    gate_held = by_name(
        halving_step(contract_rows(mid_rows[:, :half], grad_gates).astype(BF16), give_gate, 0), relative[: dp // 2]
    )
    up_held = by_name(
        halving_step(contract_rows(mid_rows[:, :half], grad_ups).astype(BF16), give_up, 0), relative[: dp // 2]
    )
    for at in range(bits - 2):
        gate_held, up_held = halve(gate_held, bits - 1 - at), halve(up_held, 1 + at)
    grad_attn, down_move, part_output, gate_held, up_held = barrier(
        (grad_attn, down_move, part_output, gate_held, up_held)
    )
    summed_output = scattered(part_output, 1)
    down_move = around((late[2] + down_move.astype(F32)).astype(BF16))
    gate_held, up_held = halve(gate_held, 1), halve(up_held, bits - 1)

    grad_qkv, gain_parts = backward_heads(
        qkv, grad_attn, lse, cosine, sine, gain_query, gain_key, heads, kv_heads
    )
    grad_qkv, down_move, gate_held, up_held, summed_down = barrier(
        (grad_qkv, down_move, gate_held, up_held, summed_down)
    )
    summed_gate, summed_up = gate_held[0], up_held[0]
    for k in range(3, parts):
        down_move = around((late[k] + down_move.astype(F32)).astype(BF16))
    layer_out = (resid + late[0] + down_move.astype(F32)).astype(BF16)

    grads_in, part_pre = [], 0.0
    for k in range(parts):
        block = lax.dynamic_slice(grad_qkv, (place(k) * rows, 0), (rows, grad_qkv.shape[1]))
        grads_in.append(contract_cols(block, w_qkv))
        wide, scale = normals[k]
        part_pre = part_pre + jnp.sum(grads_in[k] * (wide * scale), axis=0)

    def gain_filler():
        packed = jnp.concatenate([part_pre, part_mid, gain_parts[0], gain_parts[1]])
        return butterfly(packed.reshape(-1, 128)).reshape(-1)

    grad_pre_in, (part_qkv, (gain_sums, summed_output), _) = scatter_ring(
        lambda k: grads_in[k],
        (
            lambda: contract_rows(normed_full, grad_qkv).astype(BF16),
            lambda: (gain_filler(), summed_output),
        ),
    )
    summed_qkv = scattered(part_qkv, 0).astype(F32)
    summed_output = lax.psum_scatter(
        summed_output, "tensor", scatter_dimension=0, tiled=True
    ).astype(F32)
    scale_pre = normals[0][1]
    back_pre = rms_back(inputs_wide * scale_pre, scale_pre, pre_full, grad_pre_in)
    in_grad = (grad_resid + back_pre).astype(BF16)

    summed_down = summed_down.astype(F32)
    summed_gate_up = jnp.stack([summed_gate.astype(F32), summed_up.astype(F32)], axis=1)
    cuts = [w_query.shape[1], w_query.shape[1] + w_key.shape[1]]
    summed_query, summed_key, summed_value = jnp.split(summed_qkv, cuts, axis=1)

    outs, at = [], 0
    for full, size in zip((width, width, head_size, head_size), sizes):
        outs.append(lax.dynamic_slice(gain_sums, (at + mine * size,), (size,)))
        at += full
    return (
        layer_out,
        in_grad,
        summed_query,
        summed_key,
        summed_value,
        summed_output,
        summed_gate_up,
        summed_down,
        *outs,
    )


def solution(mesh):
    placed = (
        P(("dp", "tensor"), None),
        P("dp", "tensor"),
        P("dp", "tensor"),
        P("dp", "tensor"),
        P("tensor", "dp"),
        P("dp", None, "tensor"),
        P("tensor", "dp"),
        P("dp"),
        P("dp"),
        P("dp"),
        P("dp"),
        P(("dp", "tensor"), None),
    )
    return jax.shard_map(
        functools.partial(on_device, (mesh.shape["dp"], mesh.shape["tensor"])),
        mesh=mesh,
        in_specs=placed,
        out_specs=(
            P(("dp", "tensor"), None),
            P(("dp", "tensor"), None),
            P("dp", "tensor"),
            P("dp", "tensor"),
            P("dp", "tensor"),
            P("tensor", "dp"),
            P("dp", None, "tensor"),
            P("tensor", "dp"),
            P("dp"),
            P("dp"),
            P("dp"),
            P("dp"),
        ),
        check_vma=False,
    )
```

```python
import functools

import jax
import jax.numpy as jnp
from jax import lax
from jax.experimental import pallas as pl
from jax.experimental.pallas import tpu as pltpu
from jax.sharding import PartitionSpec as P


L = 1024


EPS = 1e-06
THETA = 1000000.0
F32 = jnp.float32
BF16 = jnp.bfloat16
BLOCK = 256


barrier = lax.optimization_barrier


def dot(left, right):
    return jnp.dot(left, right, preferred_element_type=F32)


def contract_rows(left, right):
    return lax.dot_general(left, right, (((0,), (0,)), ((), ())), preferred_element_type=F32)


def contract_cols(left, right):
    return lax.dot_general(left, right, (((1,), (1,)), ((), ())), preferred_element_type=F32)


def rope_tables(head_size):
    half = head_size // 2
    freq = THETA ** (-(jnp.arange(half, dtype=F32) * 2.0) / head_size)
    angle = jnp.arange(L).astype(F32)[:, None] * freq[None, :]
    cosine, sine = jnp.cos(angle), jnp.sin(angle)
    return (
        jnp.concatenate([cosine, cosine], axis=1),
        jnp.concatenate([-sine, sine], axis=1),
    )


def rms_scale(values):
    return lax.rsqrt(jnp.mean(values * values, axis=-1, keepdims=True) + EPS)


def rms_back(normal, scale, gain, grads):
    scaled = grads * gain
    inner = jnp.mean(scaled * normal, axis=-1, keepdims=True)
    return scale * (scaled - normal * inner)


def turn(values):
    return pltpu.roll(values, values.shape[-1] // 2, 1)


def causal_block(scores_t):
    keys = lax.broadcasted_iota(jnp.int32, scores_t.shape, 0)
    queries = lax.broadcasted_iota(jnp.int32, scores_t.shape, 1)
    return keys <= queries


def attention_forward(group, size, q_ref, k_ref, v_ref, cos_ref, sin_ref, gq_ref, gk_ref, out_ref, lse_ref):
    cosine, sine = cos_ref[...], sin_ref[...]
    factor = size ** (-0.5)
    keys = k_ref[...]
    keys = keys * rms_scale(keys) * gk_ref[...]
    keys = (keys * cosine + turn(keys) * sine).astype(BF16)
    values_t = v_ref[...].T.astype(BF16)
    for h in range(group):
        query = q_ref[:, h * size : (h + 1) * size]
        query = query * rms_scale(query) * gq_ref[...]
        query = (query * cosine + turn(query) * sine).astype(BF16)
        for b in range(L // BLOCK):
            lo, hi = b * BLOCK, (b + 1) * BLOCK
            scores = contract_cols(keys[:hi], query[lo:hi]) * factor
            powers = jnp.exp(scores)
            last = jnp.where(causal_block(powers[lo:]), powers[lo:], 0.0)
            powers = jnp.concatenate([powers[:lo], last], axis=0) if lo else last
            total = jnp.sum(powers, axis=0, keepdims=True)
            probs = (powers * (1.0 / total)).astype(BF16)
            mixed_t = dot(values_t[:, :hi], probs)
            out_ref[lo:hi, h * size : (h + 1) * size] = mixed_t.T.astype(BF16)
            lse_ref[0, h : h + 1, lo:hi] = jnp.log(total)


def attention_backward(
    group, size, heads, kv_heads, q_ref, k_ref, v_ref, grad_ref, lse_ref, cos_ref, sin_ref, gq_ref, gk_ref,
    out_ref, gain_ref, dk_ref, dv_ref, dq_ref,
):
    first = (pl.program_id(0) == 0) & (pl.program_id(1) == 0)

    @pl.when(first)
    def _():
        gain_ref[...] = jnp.zeros_like(gain_ref)

    at = pl.program_id(1)
    cosine, sine = cos_ref[...], sin_ref[...]
    factor = size ** (-0.5)
    raw_k = k_ref[...]
    scale_k = rms_scale(raw_k)
    normal_k = raw_k * scale_k
    keys = normal_k * gk_ref[...]
    keys = keys * cosine + turn(keys) * sine
    keys_t = keys.T.astype(BF16)
    keys = keys.astype(BF16)
    values = v_ref[...].astype(BF16)
    dk_ref[...] = jnp.zeros_like(dk_ref)
    dv_ref[...] = jnp.zeros_like(dv_ref)
    for h in range(group):
        cols = slice(h * size, (h + 1) * size)
        raw_q = q_ref[:, cols]
        scale_q = rms_scale(raw_q)
        normal_q = raw_q * scale_q
        query = normal_q * gq_ref[...]
        query = (query * cosine + turn(query) * sine).astype(BF16)
        grad = grad_ref[:, cols]
        for b in range(L // BLOCK):
            lo, hi = b * BLOCK, (b + 1) * BLOCK
            q_b, g_b = query[lo:hi], grad[lo:hi]
            scores = contract_cols(keys[:hi], q_b) * factor
            probs = jnp.exp(scores - lse_ref[0, h : h + 1, lo:hi])
            last = jnp.where(causal_block(probs[lo:]), probs[lo:], 0.0)
            probs = jnp.concatenate([probs[:lo], last], axis=0) if lo else last
            dv_ref[:hi] += dot(probs.astype(BF16), g_b)
            grad_probs = contract_cols(values[:hi], g_b)
            inner = jnp.sum(probs * grad_probs, axis=0, keepdims=True)
            grad_scores = (probs * (grad_probs - inner) * factor).astype(BF16)
            dk_ref[:hi] += dot(grad_scores, q_b)
            dq_ref[lo:hi] = dot(keys_t[:, :hi], grad_scores).T
        dq = dq_ref[...]
        dqn = dq * cosine - turn(dq) * sine
        gain_ref[0:1] += jnp.sum(dqn * normal_q, axis=0, keepdims=True)
        back = rms_back(normal_q, scale_q, gq_ref[...], dqn)
        out_ref[:, pl.ds(pl.multiple_of((at * group + h) * size, size), size)] = back.astype(BF16)
    dk = dk_ref[...]
    dkn = dk * cosine - turn(dk) * sine
    gain_ref[1:2] += jnp.sum(dkn * normal_k, axis=0, keepdims=True)
    back = rms_back(normal_k, scale_k, gk_ref[...], dkn)
    out_ref[:, pl.ds(pl.multiple_of((heads + at) * size, size), size)] = back.astype(BF16)
    out_ref[:, pl.ds(pl.multiple_of((heads + kv_heads + at) * size, size), size)] = dv_ref[...].astype(BF16)


def hidden_kernel(blocks, *refs):
    gate_refs, up_refs = refs[:blocks], refs[blocks : 2 * blocks]
    mid_ref, og_ref, down_ref, hidden_ref, grad_gate_ref, grad_up_ref, back_ref, out_ref = refs[2 * blocks :]
    gate_w = jnp.concatenate([ref[...] for ref in gate_refs], axis=0)
    up_w = jnp.concatenate([ref[...] for ref in up_refs], axis=0)
    mid, down_w = mid_ref[...], down_ref[...]
    gate = dot(mid, gate_w)
    upper = dot(mid, up_w)
    grad_hidden = contract_cols(og_ref[...], down_w)
    sigma = 1.0 / (1.0 + jnp.exp(-gate))
    silu = gate * sigma
    hidden = (silu * upper).astype(BF16)
    grad_gate = (grad_hidden * upper * sigma * (1.0 + gate * (1.0 - sigma))).astype(BF16)
    grad_up = (grad_hidden * silu).astype(BF16)
    hidden_ref[...] = hidden
    grad_gate_ref[...] = grad_gate
    grad_up_ref[...] = grad_up
    back = contract_cols(grad_gate, gate_w) + contract_cols(grad_up, up_w)
    out = dot(hidden, down_w)

    @pl.when(pl.program_id(0) == 0)
    def _():
        back_ref[...] = back
        out_ref[...] = out

    @pl.when(pl.program_id(0) > 0)
    def _():
        back_ref[...] += back
        out_ref[...] += out


def hidden_piece(mid, og, gate_blocks, up_blocks, down_w):
    rows, width = mid.shape
    units = down_w.shape[0]
    blocks = len(gate_blocks)
    tile = min(512, units)
    whole = pl.BlockSpec((rows, width), lambda j: (0, 0))
    out = pl.BlockSpec((rows, tile), lambda j: (0, j))
    block = pl.BlockSpec((width // blocks, tile), lambda j: (0, j))
    return pl.pallas_call(
        functools.partial(hidden_kernel, blocks),
        grid=(units // tile,),
        in_specs=[block] * (2 * blocks) + [whole, whole, pl.BlockSpec((tile, width), lambda j: (j, 0))],
        out_specs=(out, out, out, whole, whole),
        out_shape=tuple(jax.ShapeDtypeStruct((rows, units), BF16) for _ in range(3))
        + tuple(jax.ShapeDtypeStruct((rows, width), F32) for _ in range(2)),
        cost_estimate=pl.CostEstimate(
            flops=12 * rows * width * units,
            transcendentals=rows * units,
            bytes_accessed=6 * width * units + 12 * rows * width + 6 * rows * units,
        ),
        name="hidden_piece",
    )(*gate_blocks, *up_blocks, mid, og, down_w)


def shuffle_kernel(size, order_ref, in_ref, out_ref):
    for i in range(in_ref.shape[1] // size):
        at = pl.multiple_of(order_ref[i] * size, size)
        out_ref[:, i * size : (i + 1) * size] = in_ref[:, pl.ds(at, size)]


def shuffled(values, order):
    size = values.shape[1] // order.shape[0]
    if size % 128:
        cut = values.reshape(values.shape[0], order.shape[0], size)
        return cut[:, order].reshape(values.shape)
    whole = pl.BlockSpec(values.shape, lambda i, order: (0, 0))
    return pl.pallas_call(
        functools.partial(shuffle_kernel, size),
        grid_spec=pltpu.PrefetchScalarGridSpec(
            num_scalar_prefetch=1, grid=(1,), in_specs=[whole], out_specs=whole
        ),
        out_shape=jax.ShapeDtypeStruct(values.shape, values.dtype),
        cost_estimate=pl.CostEstimate(
            flops=0, transcendentals=0, bytes_accessed=2 * values.size * values.dtype.itemsize
        ),
        name="shuffled",
    )(order, values)


def qkv_specs(group, size, heads, kv_heads):
    return [
        pl.BlockSpec((L, group * size), lambda s, g: (s, g)),
        pl.BlockSpec((L, size), lambda s, g: (s, heads + g)),
        pl.BlockSpec((L, size), lambda s, g: (s, heads + kv_heads + g)),
    ]


def forward_heads(qkv, cosine, sine, gain_q, gain_k, heads, kv_heads):
    rows, size, group = qkv.shape[0], cosine.shape[1], heads // kv_heads
    fixed = pl.BlockSpec((L, size), lambda s, g: (0, 0))
    gain = pl.BlockSpec((1, size), lambda s, g: (0, 0))
    return pl.pallas_call(
        functools.partial(attention_forward, group, size),
        grid=(rows // L, kv_heads),
        in_specs=qkv_specs(group, size, heads, kv_heads) + [fixed, fixed, gain, gain],
        out_specs=(
            pl.BlockSpec((L, group * size), lambda s, g: (s, g)),
            pl.BlockSpec((1, group, L), lambda s, g: (s * kv_heads + g, 0, 0)),
        ),
        out_shape=(
            jax.ShapeDtypeStruct((rows, heads * size), BF16),
            jax.ShapeDtypeStruct((rows // L * kv_heads, group, L), F32),
        ),
        cost_estimate=pl.CostEstimate(
            flops=4 * heads * rows * L * size,
            transcendentals=heads * rows * L,
            bytes_accessed=rows * (heads + 2 * kv_heads) * size * 4 + rows * heads * size * 2,
        ),
        name="attention_forward",
    )(qkv, qkv, qkv, cosine, sine, gain_q, gain_k)


def backward_heads(qkv, grad, lse, cosine, sine, gain_q, gain_k, heads, kv_heads):
    rows, size, group = qkv.shape[0], cosine.shape[1], heads // kv_heads
    width = (heads + 2 * kv_heads) * size
    fixed = pl.BlockSpec((L, size), lambda s, g: (0, 0))
    gain = pl.BlockSpec((1, size), lambda s, g: (0, 0))
    return pl.pallas_call(
        functools.partial(attention_backward, group, size, heads, kv_heads),
        grid=(rows // L, kv_heads),
        in_specs=qkv_specs(group, size, heads, kv_heads)
        + [
            pl.BlockSpec((L, group * size), lambda s, g: (s, g)),
            pl.BlockSpec((1, group, L), lambda s, g: (s * kv_heads + g, 0, 0)),
            fixed,
            fixed,
            gain,
            gain,
        ],
        out_specs=(
            pl.BlockSpec((L, width), lambda s, g: (s, 0)),
            pl.BlockSpec((2, size), lambda s, g: (0, 0)),
        ),
        out_shape=(
            jax.ShapeDtypeStruct((rows, width), BF16),
            jax.ShapeDtypeStruct((2, size), F32),
        ),
        scratch_shapes=[pltpu.VMEM((L, size), F32)] * 3,
        cost_estimate=pl.CostEstimate(
            flops=10 * heads * rows * L * size,
            transcendentals=heads * rows * L,
            bytes_accessed=rows * width * 6 + rows * heads * size * 2,
        ),
        name="attention_backward",
    )(qkv, qkv, qkv, grad, lse, cosine, sine, gain_q, gain_k)


def on_device(
    devices,
    layer_in,
    w_query,
    w_key,
    w_value,
    w_output,
    w_gate_up,
    w_down,
    pre_gain,
    mid_gain,
    query_gain,
    key_gain,
    out_grad,
):
    dp, parts = devices
    ring = [(i, (i + 1) % parts) for i in range(parts)]
    me = lax.axis_index("tensor")
    mine = lax.axis_index("dp")
    rows, width = layer_in.shape
    all_rows = rows * parts
    head_size = query_gain.shape[0] * dp
    heads = w_query.shape[1] // head_size
    kv_heads = w_key.shape[1] // head_size

    def place(k):
        return (me + parts - k) % parts

    def around(block):
        return lax.ppermute(block, "tensor", ring)

    def gather_ring(block):
        blocks = [block]
        for _ in range(1, parts):
            blocks.append(around(blocks[-1]))
        return blocks

    def scatter_ring(part, fillers=(), tied=None):
        order = list(range(1, parts)) + [0]
        made = []
        total = part(order[0])
        for j, k in enumerate(order[1:]):
            moving = around(total.astype(BF16))
            ahead = part(k)
            new = fillers[j]() if j < len(fillers) else ()
            moving, ahead, new = barrier((moving, ahead, new))
            total = ahead + moving.astype(F32)
            made.append(new)
            if tied is not None and isinstance(new, tuple) and len(new) > 1:
                tied.append(new[1])
        return total, made

    def scattered(part, axis):
        return lax.psum_scatter(part, "dp", scatter_dimension=axis, tiled=True)

    bits = dp.bit_length() - 1

    def swap(block, bit):
        return lax.ppermute(block, "dp", [(i, i ^ (1 << bit)) for i in range(dp)])

    near_last = list(range(1, bits)) + [0]
    relative = [0]
    for bit in near_last:
        relative = relative + [r | (1 << bit) for r in relative]

    def doubling_step(held, bit):
        return {**held, **{r | (1 << bit): swap(block, bit) for r, block in held.items()}}

    def halving_step(keep, give, bit):
        return (keep.astype(F32) + swap(give, bit).astype(F32)).astype(BF16)

    def halve(held, bit):
        keep = [r for r in held if not (r >> bit) & 1]
        far = swap(jnp.concatenate([held[r | (1 << bit)] for r in keep], axis=0), bit)
        size = far.shape[0] // len(keep)
        return {
            r: (held[r].astype(F32) + far[i * size : (i + 1) * size].astype(F32)).astype(BF16)
            for i, r in enumerate(keep)
        }

    def by_name(block, names):
        size = block.shape[0] // len(names)
        return {r: block[i * size : (i + 1) * size] for i, r in enumerate(names)}

    def butterfly(values):
        for axis, size in (("dp", dp), ("tensor", parts)):
            for bit in range(size.bit_length() - 1):
                values = values + lax.ppermute(values, axis, [(i, i ^ (1 << bit)) for i in range(size)])
        return values

    sizes = (pre_gain.shape[0], mid_gain.shape[0], query_gain.shape[0], key_gain.shape[0])
    used = sum(sizes)
    packed = jnp.concatenate([pre_gain, mid_gain, query_gain, key_gain])
    packed = jnp.pad(packed, (0, -used % 128)).reshape(1, -1)
    w_qkv = lax.all_gather(jnp.concatenate([w_query, w_key, w_value], axis=1), "dp", axis=0, tiled=True)
    xs = [layer_in, around(layer_in)]
    steps = list(zip(near_last, near_last[:-1][::-1] + near_last[-1:]))
    blocks = [{0: w_gate_up[:, 0]}, {0: w_gate_up[:, 1]}]

    def double(hop):
        if steps:
            for i, bit in enumerate(steps.pop(0)):
                blocks[i] = doubling_step(blocks[i], bit)
            blocks[:], hop = barrier((blocks, hop))
        return hop

    cosine, sine = rope_tables(head_size)
    xs[1], cosine, sine = barrier((xs[1], cosine, sine))
    w_output, packed, _ = barrier((w_output, packed, xs[1]))
    output_w = lax.all_gather(w_output, "tensor", axis=0, tiled=True)
    gains = lax.all_gather(packed, "dp", axis=0, tiled=True).astype(F32)
    starts = [sum(sizes[:i]) for i in range(5)]
    pre_full, mid_full, gain_query, gain_key = (
        gains[:, lo:hi].reshape(1, -1) for lo, hi in zip(starts, starts[1:])
    )

    normals = []
    qkv = jnp.zeros((all_rows, w_qkv.shape[1]), F32)
    normed_full = jnp.zeros((all_rows, width), BF16)
    for k in range(parts):
        if 0 < k < parts - 1:
            xs.append(around(xs[k]))
        wide = xs[k].astype(F32)
        scale = rms_scale(wide)
        normals.append((wide, scale))
        normed = (wide * scale * pre_full).astype(BF16)
        at = (place(k) * rows, 0)
        normed_full = lax.dynamic_update_slice(normed_full, normed, at)
        qkv = lax.dynamic_update_slice(qkv, dot(normed, w_qkv), at)
        if k == 1:
            xs[2] = double(xs[2])
            qkv, normed_full, xs[2] = barrier((qkv, normed_full, xs[2]))
        if k == parts - 2:
            qkv, normed_full, xs[-1], output_w = barrier((qkv, normed_full, xs[-1], output_w))
            output_w = lax.all_gather(output_w, "dp", axis=1, tiled=True)

    down_w = lax.all_gather(w_down, "dp", axis=1, tiled=True)
    first_og, _ = barrier((out_grad, xs[-1]))
    ogs = [out_grad, around(first_og)]
    attention, lse = forward_heads(qkv, cosine, sine, gain_query, gain_key, heads, kv_heads)
    attention, ogs[1] = barrier((attention, ogs[1]))
    ogs.append(around(ogs[1]))
    mixed = lax.all_to_all(
        attention.reshape(parts, rows, heads * head_size), "tensor", 0, 0, tiled=True
    )
    mixed = mixed.transpose(1, 0, 2).reshape(rows, parts * heads * head_size)
    mixed, ogs[-1] = barrier((mixed, ogs[-1]))
    while len(steps) > 1:
        mixed = double(mixed)
    for k in range(2, parts - 1):
        ogs.append(around(ogs[k]))
    inputs_wide = normals[0][0]
    resid = inputs_wide + dot(mixed, output_w)
    scale_mid = rms_scale(resid)
    normal_mid = resid * scale_mid
    mids = gather_ring(
        shuffled((normal_mid * mid_full).astype(BF16), mine ^ jnp.asarray(relative, jnp.int32))
    )
    if parts > 1:
        mids[1] = double(mids[1])
    gate_blocks, up_blocks = ([held[r] for r in relative] for held in blocks)
    pieces = {}

    def piece(k):
        pieces[k] = hidden_piece(mids[k], ogs[k], gate_blocks, up_blocks, down_w)
        return pieces[k][3]

    def rows_of(blocks):
        return jnp.concatenate(blocks, axis=0)

    def column(i):
        return rows_of([pieces[k][i] for k in range(parts)])

    half = width // 2
    piece(1)
    down_parts = []

    def down_filler():
        down_parts.append(contract_rows(column(0), rows_of(ogs)).astype(BF16))
        return down_parts[0]

    grad_mid_in, _ = scatter_ring(piece, [tuple] * (parts - 2) + [down_filler])
    summed_down = scattered(down_parts[0], 1)
    mid_rows, grad_gates, grad_ups = rows_of(mids), column(1), column(2)
    gives = [contract_rows(mid_rows[:, half:], grads).astype(BF16) for grads in (grad_gates, grad_ups)]
    back_order = [relative.index(r) for r in range(dp)]
    grad_mid_in = shuffled(
        grad_mid_in, jnp.asarray(back_order, jnp.int32)[mine ^ jnp.arange(dp, dtype=jnp.int32)]
    )
    grad_resid = out_grad.astype(F32) + rms_back(normal_mid, scale_mid, mid_full, grad_mid_in)
    part_mid = jnp.sum(grad_mid_in * normal_mid, axis=0)
    grad_resid_b = grad_resid.astype(BF16)

    late = barrier(([pieces[k][4] for k in range(parts)], grad_resid_b))[0]
    down_move = around(late[1].astype(BF16))
    grad_mixed = contract_cols(grad_resid_b, output_w).astype(BF16)
    grad_mixed = grad_mixed.reshape(rows, parts, heads * head_size).transpose(1, 0, 2)
    grad_attn = lax.all_to_all(grad_mixed, "tensor", 0, 0, tiled=True)
    grad_attn = grad_attn.reshape(all_rows, heads * head_size)
    mixed, grad_resid_b, _ = barrier((mixed, grad_resid_b, grad_mixed))
    part_output = contract_rows(mixed, grad_resid_b).astype(BF16)
    summed_output = scattered(part_output, 1)
    mid_rows, grad_gates, grad_ups, _, _ = barrier((mid_rows, grad_gates, grad_ups, grad_mixed, part_output))
    held = []
    for give, grads in zip(gives, (grad_gates, grad_ups)):
        keep = contract_rows(mid_rows[:, :half], grads).astype(BF16)
        held.append(by_name(halving_step(keep, give, 0), relative[: dp // 2]))
    grad_attn, down_move, held = barrier((grad_attn, down_move, held))
    down_move = around((late[2] + down_move.astype(F32)).astype(BF16))
    held = [halve(held[0], bits - 1), halve(held[1], 1)]

    grad_qkv, gain_parts = backward_heads(
        qkv, grad_attn, lse, cosine, sine, gain_query, gain_key, heads, kv_heads
    )
    grad_qkv, summed_down = barrier((grad_qkv, summed_down))

    grads_in, part_pre = [], 0.0
    for k in range(parts):
        block = lax.dynamic_slice(grad_qkv, (place(k) * rows, 0), (rows, grad_qkv.shape[1]))
        grads_in.append(contract_cols(block, w_qkv))
        wide, scale = normals[k]
        part_pre = part_pre + jnp.sum(grads_in[k] * (wide * scale), axis=0)

    def gain_filler():
        packed = jnp.concatenate([part_pre, part_mid, gain_parts[0], gain_parts[1]])
        return butterfly(packed.reshape(-1, 128)).reshape(-1)

    part_qkv = contract_rows(normed_full, grad_qkv).astype(BF16)
    moves = [down_move, held]

    def first_filler():
        return part_qkv, moves, summed_output

    def second_filler():
        return gain_filler(), moves

    def step_moves(last):
        at = len(moves_done) + 1
        moves_done.append(last)
        down_move, held = last
        if 2 + at < parts:
            down_move = around((late[2 + at] + down_move.astype(F32)).astype(BF16))
        if at < bits - 1:
            held = [halve(held[0], bits - 1 - at), halve(held[1], 1 + at)]
        return [down_move, held]

    moves_done, tied = [], []

    def filler(make):
        def run():
            nonlocal moves
            if tied:
                moves = step_moves(tied[-1])
            return make()

        return run

    grad_pre_in, made = scatter_ring(lambda k: grads_in[k], (filler(first_filler), filler(second_filler)), tied)
    _, _, summed_output = made[0]
    gain_sums, (down_move, held) = made[1]
    for at in range(len(moves_done) + 1, max(bits - 1, parts - 2)):
        down_move, held = step_moves([down_move, held])
    summed_gate, summed_up = (h[0] for h in held)
    layer_out = (resid + late[0] + down_move.astype(F32)).astype(BF16)
    summed_output = lax.psum_scatter(
        summed_output, "tensor", scatter_dimension=0, tiled=True
    ).astype(F32)
    summed_qkv = scattered(part_qkv, 0).astype(F32)
    scale_pre = normals[0][1]
    back_pre = rms_back(inputs_wide * scale_pre, scale_pre, pre_full, grad_pre_in)
    in_grad = (grad_resid + back_pre).astype(BF16)

    summed_down = summed_down.astype(F32)
    summed_gate_up = jnp.stack([summed_gate.astype(F32), summed_up.astype(F32)], axis=1)
    cuts = [w_query.shape[1], w_query.shape[1] + w_key.shape[1]]
    summed_query, summed_key, summed_value = jnp.split(summed_qkv, cuts, axis=1)

    outs, at = [], 0
    for full, size in zip((width, width, head_size, head_size), sizes):
        outs.append(lax.dynamic_slice(gain_sums, (at + mine * size,), (size,)))
        at += full
    return (
        layer_out,
        in_grad,
        summed_query,
        summed_key,
        summed_value,
        summed_output,
        summed_gate_up,
        summed_down,
        *outs,
    )


def solution(mesh):
    placed = (
        P(("dp", "tensor"), None),
        P("dp", "tensor"),
        P("dp", "tensor"),
        P("dp", "tensor"),
        P("tensor", "dp"),
        P("dp", None, "tensor"),
        P("tensor", "dp"),
        P("dp"),
        P("dp"),
        P("dp"),
        P("dp"),
        P(("dp", "tensor"), None),
    )
    return jax.shard_map(
        functools.partial(on_device, (mesh.shape["dp"], mesh.shape["tensor"])),
        mesh=mesh,
        in_specs=placed,
        out_specs=(
            P(("dp", "tensor"), None),
            P(("dp", "tensor"), None),
            P("dp", "tensor"),
            P("dp", "tensor"),
            P("dp", "tensor"),
            P("tensor", "dp"),
            P("dp", None, "tensor"),
            P("tensor", "dp"),
            P("dp"),
            P("dp"),
            P("dp"),
            P("dp"),
        ),
        check_vma=False,
    )
```

```python
import functools

import jax
import jax.numpy as jnp
from jax import lax
from jax.experimental import pallas as pl
from jax.experimental.pallas import tpu as pltpu
from jax.sharding import PartitionSpec as P


L = 1024


EPS = 1e-06
THETA = 1000000.0
F32 = jnp.float32
BF16 = jnp.bfloat16
BLOCK = 256


barrier = lax.optimization_barrier


def dot(left, right):
    return jnp.dot(left, right, preferred_element_type=F32)


def contract_rows(left, right):
    return lax.dot_general(left, right, (((0,), (0,)), ((), ())), preferred_element_type=F32)


def contract_cols(left, right):
    return lax.dot_general(left, right, (((1,), (1,)), ((), ())), preferred_element_type=F32)


def rope_tables(head_size):
    half = head_size // 2
    freq = THETA ** (-(jnp.arange(half, dtype=F32) * 2.0) / head_size)
    angle = jnp.arange(L).astype(F32)[:, None] * freq[None, :]
    cosine, sine = jnp.cos(angle), jnp.sin(angle)
    return (
        jnp.concatenate([cosine, cosine], axis=1),
        jnp.concatenate([-sine, sine], axis=1),
    )


def rms_scale(values):
    return lax.rsqrt(jnp.mean(values * values, axis=-1, keepdims=True) + EPS)


def rms_back(normal, scale, gain, grads):
    scaled = grads * gain
    inner = jnp.mean(scaled * normal, axis=-1, keepdims=True)
    return scale * (scaled - normal * inner)


def turn(values):
    return pltpu.roll(values, values.shape[-1] // 2, 1)


def causal_block(scores_t):
    keys = lax.broadcasted_iota(jnp.int32, scores_t.shape, 0)
    queries = lax.broadcasted_iota(jnp.int32, scores_t.shape, 1)
    return keys <= queries


def attention_forward(group, size, q_ref, k_ref, v_ref, cos_ref, sin_ref, gq_ref, gk_ref, out_ref, lse_ref):
    cosine, sine = cos_ref[...], sin_ref[...]
    factor = size ** (-0.5)
    keys = k_ref[...]
    keys = keys * rms_scale(keys) * gk_ref[...]
    keys = (keys * cosine + turn(keys) * sine).astype(BF16)
    values_t = v_ref[...].T.astype(BF16)
    for h in range(group):
        query = q_ref[:, h * size : (h + 1) * size]
        query = query * rms_scale(query) * gq_ref[...]
        query = (query * cosine + turn(query) * sine).astype(BF16)
        for b in range(L // BLOCK):
            lo, hi = b * BLOCK, (b + 1) * BLOCK
            scores = contract_cols(keys[:hi], query[lo:hi]) * factor
            powers = jnp.exp(scores)
            last = jnp.where(causal_block(powers[lo:]), powers[lo:], 0.0)
            powers = jnp.concatenate([powers[:lo], last], axis=0) if lo else last
            total = jnp.sum(powers, axis=0, keepdims=True)
            probs = (powers * (1.0 / total)).astype(BF16)
            mixed_t = dot(values_t[:, :hi], probs)
            out_ref[lo:hi, h * size : (h + 1) * size] = mixed_t.T.astype(BF16)
            lse_ref[0, h : h + 1, lo:hi] = jnp.log(total)


def attention_backward(
    group, size, heads, kv_heads, q_ref, k_ref, v_ref, grad_ref, lse_ref, cos_ref, sin_ref, gq_ref, gk_ref,
    out_ref, gain_ref, dk_ref, dv_ref, dq_ref,
):
    first = (pl.program_id(0) == 0) & (pl.program_id(1) == 0)

    @pl.when(first)
    def _():
        gain_ref[...] = jnp.zeros_like(gain_ref)

    at = pl.program_id(1)
    cosine, sine = cos_ref[...], sin_ref[...]
    factor = size ** (-0.5)
    raw_k = k_ref[...]
    scale_k = rms_scale(raw_k)
    normal_k = raw_k * scale_k
    keys = normal_k * gk_ref[...]
    keys = keys * cosine + turn(keys) * sine
    keys_t = keys.T.astype(BF16)
    keys = keys.astype(BF16)
    values = v_ref[...].astype(BF16)
    dk_ref[...] = jnp.zeros_like(dk_ref)
    dv_ref[...] = jnp.zeros_like(dv_ref)
    for h in range(group):
        cols = slice(h * size, (h + 1) * size)
        raw_q = q_ref[:, cols]
        scale_q = rms_scale(raw_q)
        normal_q = raw_q * scale_q
        query = normal_q * gq_ref[...]
        query = (query * cosine + turn(query) * sine).astype(BF16)
        grad = grad_ref[:, cols]
        for b in range(L // BLOCK):
            lo, hi = b * BLOCK, (b + 1) * BLOCK
            q_b, g_b = query[lo:hi], grad[lo:hi]
            scores = contract_cols(keys[:hi], q_b) * factor
            probs = jnp.exp(scores - lse_ref[0, h : h + 1, lo:hi])
            last = jnp.where(causal_block(probs[lo:]), probs[lo:], 0.0)
            probs = jnp.concatenate([probs[:lo], last], axis=0) if lo else last
            dv_ref[:hi] += dot(probs.astype(BF16), g_b)
            grad_probs = contract_cols(values[:hi], g_b)
            inner = jnp.sum(probs * grad_probs, axis=0, keepdims=True)
            grad_scores = (probs * (grad_probs - inner) * factor).astype(BF16)
            dk_ref[:hi] += dot(grad_scores, q_b)
            dq_ref[lo:hi] = dot(keys_t[:, :hi], grad_scores).T
        dq = dq_ref[...]
        dqn = dq * cosine - turn(dq) * sine
        gain_ref[0:1] += jnp.sum(dqn * normal_q, axis=0, keepdims=True)
        back = rms_back(normal_q, scale_q, gq_ref[...], dqn)
        out_ref[:, pl.ds(pl.multiple_of((at * group + h) * size, size), size)] = back.astype(BF16)
    dk = dk_ref[...]
    dkn = dk * cosine - turn(dk) * sine
    gain_ref[1:2] += jnp.sum(dkn * normal_k, axis=0, keepdims=True)
    back = rms_back(normal_k, scale_k, gk_ref[...], dkn)
    out_ref[:, pl.ds(pl.multiple_of((heads + at) * size, size), size)] = back.astype(BF16)
    out_ref[:, pl.ds(pl.multiple_of((heads + kv_heads + at) * size, size), size)] = dv_ref[...].astype(BF16)


def hidden_kernel(blocks, *refs):
    gate_refs, up_refs = refs[:blocks], refs[blocks : 2 * blocks]
    mid_ref, og_ref, down_ref, hidden_ref, grad_gate_ref, grad_up_ref, back_ref, out_ref = refs[2 * blocks :]
    gate_w = jnp.concatenate([ref[...] for ref in gate_refs], axis=0)
    up_w = jnp.concatenate([ref[...] for ref in up_refs], axis=0)
    mid, down_w = mid_ref[...], down_ref[...]
    gate = dot(mid, gate_w)
    upper = dot(mid, up_w)
    grad_hidden = contract_cols(og_ref[...], down_w)
    sigma = 1.0 / (1.0 + jnp.exp(-gate))
    silu = gate * sigma
    hidden = (silu * upper).astype(BF16)
    grad_gate = (grad_hidden * upper * sigma * (1.0 + gate * (1.0 - sigma))).astype(BF16)
    grad_up = (grad_hidden * silu).astype(BF16)
    hidden_ref[...] = hidden
    grad_gate_ref[...] = grad_gate
    grad_up_ref[...] = grad_up
    back = contract_cols(grad_gate, gate_w) + contract_cols(grad_up, up_w)
    out = dot(hidden, down_w)

    @pl.when(pl.program_id(0) == 0)
    def _():
        back_ref[...] = back
        out_ref[...] = out

    @pl.when(pl.program_id(0) > 0)
    def _():
        back_ref[...] += back
        out_ref[...] += out


def hidden_piece(mid, og, gate_blocks, up_blocks, down_w):
    rows, width = mid.shape
    units = down_w.shape[0]
    blocks = len(gate_blocks)
    tile = min(512, units)
    whole = pl.BlockSpec((rows, width), lambda j: (0, 0))
    out = pl.BlockSpec((rows, tile), lambda j: (0, j))
    block = pl.BlockSpec((width // blocks, tile), lambda j: (0, j))
    return pl.pallas_call(
        functools.partial(hidden_kernel, blocks),
        grid=(units // tile,),
        in_specs=[block] * (2 * blocks) + [whole, whole, pl.BlockSpec((tile, width), lambda j: (j, 0))],
        out_specs=(out, out, out, whole, whole),
        out_shape=tuple(jax.ShapeDtypeStruct((rows, units), BF16) for _ in range(3))
        + tuple(jax.ShapeDtypeStruct((rows, width), F32) for _ in range(2)),
        cost_estimate=pl.CostEstimate(
            flops=12 * rows * width * units,
            transcendentals=rows * units,
            bytes_accessed=6 * width * units + 12 * rows * width + 6 * rows * units,
        ),
        name="hidden_piece",
    )(*gate_blocks, *up_blocks, mid, og, down_w)


def shuffle_kernel(size, order_ref, in_ref, out_ref):
    for i in range(in_ref.shape[1] // size):
        at = pl.multiple_of(order_ref[i] * size, size)
        out_ref[:, i * size : (i + 1) * size] = in_ref[:, pl.ds(at, size)]


def shuffled(values, order):
    size = values.shape[1] // order.shape[0]
    if size % 128:
        cut = values.reshape(values.shape[0], order.shape[0], size)
        return cut[:, order].reshape(values.shape)
    whole = pl.BlockSpec(values.shape, lambda i, order: (0, 0))
    return pl.pallas_call(
        functools.partial(shuffle_kernel, size),
        grid_spec=pltpu.PrefetchScalarGridSpec(
            num_scalar_prefetch=1, grid=(1,), in_specs=[whole], out_specs=whole
        ),
        out_shape=jax.ShapeDtypeStruct(values.shape, values.dtype),
        cost_estimate=pl.CostEstimate(
            flops=0, transcendentals=0, bytes_accessed=2 * values.size * values.dtype.itemsize
        ),
        name="shuffled",
    )(order, values)


def qkv_specs(group, size, heads, kv_heads):
    return [
        pl.BlockSpec((L, group * size), lambda s, g: (s, g)),
        pl.BlockSpec((L, size), lambda s, g: (s, heads + g)),
        pl.BlockSpec((L, size), lambda s, g: (s, heads + kv_heads + g)),
    ]


def forward_heads(qkv, cosine, sine, gain_q, gain_k, heads, kv_heads):
    rows, size, group = qkv.shape[0], cosine.shape[1], heads // kv_heads
    fixed = pl.BlockSpec((L, size), lambda s, g: (0, 0))
    gain = pl.BlockSpec((1, size), lambda s, g: (0, 0))
    return pl.pallas_call(
        functools.partial(attention_forward, group, size),
        grid=(rows // L, kv_heads),
        in_specs=qkv_specs(group, size, heads, kv_heads) + [fixed, fixed, gain, gain],
        out_specs=(
            pl.BlockSpec((L, group * size), lambda s, g: (s, g)),
            pl.BlockSpec((1, group, L), lambda s, g: (s * kv_heads + g, 0, 0)),
        ),
        out_shape=(
            jax.ShapeDtypeStruct((rows, heads * size), BF16),
            jax.ShapeDtypeStruct((rows // L * kv_heads, group, L), F32),
        ),
        cost_estimate=pl.CostEstimate(
            flops=4 * heads * rows * L * size,
            transcendentals=heads * rows * L,
            bytes_accessed=rows * (heads + 2 * kv_heads) * size * 4 + rows * heads * size * 2,
        ),
        name="attention_forward",
    )(qkv, qkv, qkv, cosine, sine, gain_q, gain_k)


def backward_heads(qkv, grad, lse, cosine, sine, gain_q, gain_k, heads, kv_heads):
    rows, size, group = qkv.shape[0], cosine.shape[1], heads // kv_heads
    width = (heads + 2 * kv_heads) * size
    fixed = pl.BlockSpec((L, size), lambda s, g: (0, 0))
    gain = pl.BlockSpec((1, size), lambda s, g: (0, 0))
    return pl.pallas_call(
        functools.partial(attention_backward, group, size, heads, kv_heads),
        grid=(rows // L, kv_heads),
        in_specs=qkv_specs(group, size, heads, kv_heads)
        + [
            pl.BlockSpec((L, group * size), lambda s, g: (s, g)),
            pl.BlockSpec((1, group, L), lambda s, g: (s * kv_heads + g, 0, 0)),
            fixed,
            fixed,
            gain,
            gain,
        ],
        out_specs=(
            pl.BlockSpec((L, width), lambda s, g: (s, 0)),
            pl.BlockSpec((2, size), lambda s, g: (0, 0)),
        ),
        out_shape=(
            jax.ShapeDtypeStruct((rows, width), BF16),
            jax.ShapeDtypeStruct((2, size), F32),
        ),
        scratch_shapes=[pltpu.VMEM((L, size), F32)] * 3,
        cost_estimate=pl.CostEstimate(
            flops=10 * heads * rows * L * size,
            transcendentals=heads * rows * L,
            bytes_accessed=rows * width * 6 + rows * heads * size * 2,
        ),
        name="attention_backward",
    )(qkv, qkv, qkv, grad, lse, cosine, sine, gain_q, gain_k)


def on_device(
    devices,
    layer_in,
    w_query,
    w_key,
    w_value,
    w_output,
    w_gate_up,
    w_down,
    pre_gain,
    mid_gain,
    query_gain,
    key_gain,
    out_grad,
):
    dp, parts = devices
    ring = [(i, (i + 1) % parts) for i in range(parts)]
    me = lax.axis_index("tensor")
    mine = lax.axis_index("dp")
    rows, width = layer_in.shape
    all_rows = rows * parts
    head_size = query_gain.shape[0] * dp
    heads = w_query.shape[1] // head_size
    kv_heads = w_key.shape[1] // head_size

    def place(k):
        return (me + parts - k) % parts

    def around(block):
        return lax.ppermute(block, "tensor", ring)

    def gather_ring(block):
        blocks = [block]
        for _ in range(1, parts):
            blocks.append(around(blocks[-1]))
        return blocks

    def scatter_ring(part, fillers=(), tied=None):
        order = list(range(1, parts)) + [0]
        made = []
        total = part(order[0])
        for j, k in enumerate(order[1:]):
            moving = around(total.astype(BF16))
            ahead = part(k)
            new = fillers[j]() if j < len(fillers) else ()
            moving, ahead, new = barrier((moving, ahead, new))
            total = ahead + moving.astype(F32)
            made.append(new)
            if tied is not None and isinstance(new, tuple) and len(new) > 1:
                tied.append(new[1])
        return total, made

    def scattered(part, axis):
        return lax.psum_scatter(part, "dp", scatter_dimension=axis, tiled=True)

    bits = dp.bit_length() - 1

    def swap(block, bit):
        return lax.ppermute(block, "dp", [(i, i ^ (1 << bit)) for i in range(dp)])

    near_last = list(range(1, bits)) + [0]
    relative = [0]
    for bit in near_last:
        relative = relative + [r | (1 << bit) for r in relative]

    def doubling_step(held, bit):
        return {**held, **{r | (1 << bit): swap(block, bit) for r, block in held.items()}}

    def halving_step(keep, give, bit):
        return (keep.astype(F32) + swap(give, bit).astype(F32)).astype(BF16)

    def halve(held, bit):
        keep = [r for r in held if not (r >> bit) & 1]
        far = swap(jnp.concatenate([held[r | (1 << bit)] for r in keep], axis=0), bit)
        size = far.shape[0] // len(keep)
        return {
            r: (held[r].astype(F32) + far[i * size : (i + 1) * size].astype(F32)).astype(BF16)
            for i, r in enumerate(keep)
        }

    def by_name(block, names):
        size = block.shape[0] // len(names)
        return {r: block[i * size : (i + 1) * size] for i, r in enumerate(names)}

    def butterfly(values):
        for axis, size in (("dp", dp), ("tensor", parts)):
            for bit in range(size.bit_length() - 1):
                values = values + lax.ppermute(values, axis, [(i, i ^ (1 << bit)) for i in range(size)])
        return values

    sizes = (pre_gain.shape[0], mid_gain.shape[0], query_gain.shape[0], key_gain.shape[0])
    used = sum(sizes)
    packed = jnp.concatenate([pre_gain, mid_gain, query_gain, key_gain])
    packed = jnp.pad(packed, (0, -used % 128)).reshape(1, -1)
    w_qkv = lax.all_gather(jnp.concatenate([w_query, w_key, w_value], axis=1), "dp", axis=0, tiled=True)
    xs = [layer_in, around(layer_in)]
    steps = list(zip(near_last, near_last[:-1][::-1] + near_last[-1:]))
    blocks = [{0: w_gate_up[:, 0]}, {0: w_gate_up[:, 1]}]

    def double(hop):
        if steps:
            for i, bit in enumerate(steps.pop(0)):
                blocks[i] = doubling_step(blocks[i], bit)
            blocks[:], hop = barrier((blocks, hop))
        return hop

    cosine, sine = rope_tables(head_size)
    xs[1], cosine, sine = barrier((xs[1], cosine, sine))
    w_output, packed, _ = barrier((w_output, packed, xs[1]))
    output_w = lax.all_gather(w_output, "tensor", axis=0, tiled=True)
    gains = lax.all_gather(packed, "dp", axis=0, tiled=True).astype(F32)
    starts = [sum(sizes[:i]) for i in range(5)]
    pre_full, mid_full, gain_query, gain_key = (
        gains[:, lo:hi].reshape(1, -1) for lo, hi in zip(starts, starts[1:])
    )

    normals = []
    qkv = jnp.zeros((all_rows, w_qkv.shape[1]), F32)
    normed_full = jnp.zeros((all_rows, width), BF16)
    for k in range(parts):
        if 0 < k < parts - 1:
            xs.append(around(xs[k]))
        wide = xs[k].astype(F32)
        scale = rms_scale(wide)
        normals.append((wide, scale))
        normed = (wide * scale * pre_full).astype(BF16)
        at = (place(k) * rows, 0)
        normed_full = lax.dynamic_update_slice(normed_full, normed, at)
        qkv = lax.dynamic_update_slice(qkv, dot(normed, w_qkv), at)
        if k == 1:
            xs[2] = double(xs[2])
        if k == parts - 2:
            qkv, normed_full, xs[-1], output_w = barrier((qkv, normed_full, xs[-1], output_w))
            output_w = lax.all_gather(output_w, "dp", axis=1, tiled=True)

    down_w = lax.all_gather(w_down, "dp", axis=1, tiled=True)
    first_og, _ = barrier((out_grad, xs[-1]))
    ogs = [out_grad, around(first_og)]
    attention, lse = forward_heads(qkv, cosine, sine, gain_query, gain_key, heads, kv_heads)
    attention, ogs[1] = barrier((attention, ogs[1]))
    ogs.append(around(ogs[1]))
    mixed = lax.all_to_all(
        attention.reshape(parts, rows, heads * head_size), "tensor", 0, 0, tiled=True
    )
    mixed = mixed.transpose(1, 0, 2).reshape(rows, parts * heads * head_size)
    mixed, ogs[-1] = barrier((mixed, ogs[-1]))
    while len(steps) > 1:
        mixed = double(mixed)
    for k in range(2, parts - 1):
        ogs.append(around(ogs[k]))
    inputs_wide = normals[0][0]
    resid = inputs_wide + dot(mixed, output_w)
    scale_mid = rms_scale(resid)
    normal_mid = resid * scale_mid
    mids = gather_ring(
        shuffled((normal_mid * mid_full).astype(BF16), mine ^ jnp.asarray(relative, jnp.int32))
    )
    if parts > 1:
        mids[1] = double(mids[1])
    gate_blocks, up_blocks = ([held[r] for r in relative] for held in blocks)
    pieces = {}

    def piece(k):
        pieces[k] = hidden_piece(mids[k], ogs[k], gate_blocks, up_blocks, down_w)
        return pieces[k][3]

    def rows_of(blocks):
        return jnp.concatenate(blocks, axis=0)

    def column(i):
        return rows_of([pieces[k][i] for k in range(parts)])

    half = width // 2
    piece(1)
    down_parts = []

    def down_filler():
        down_parts.append(contract_rows(column(0), rows_of(ogs)).astype(BF16))
        return down_parts[0]

    grad_mid_in, _ = scatter_ring(piece, [tuple] * (parts - 2) + [down_filler])
    summed_down = scattered(down_parts[0], 1)
    mid_rows, grad_gates, grad_ups = rows_of(mids), column(1), column(2)
    gives = [contract_rows(mid_rows[:, half:], grads).astype(BF16) for grads in (grad_gates, grad_ups)]
    back_order = [relative.index(r) for r in range(dp)]
    grad_mid_in = shuffled(
        grad_mid_in, jnp.asarray(back_order, jnp.int32)[mine ^ jnp.arange(dp, dtype=jnp.int32)]
    )
    grad_resid = out_grad.astype(F32) + rms_back(normal_mid, scale_mid, mid_full, grad_mid_in)
    part_mid = jnp.sum(grad_mid_in * normal_mid, axis=0)
    grad_resid_b = grad_resid.astype(BF16)

    late = barrier(([pieces[k][4] for k in range(parts)], grad_resid_b))[0]
    down_move = around(late[1].astype(BF16))
    grad_mixed = contract_cols(grad_resid_b, output_w).astype(BF16)
    grad_mixed = grad_mixed.reshape(rows, parts, heads * head_size).transpose(1, 0, 2)
    grad_attn = lax.all_to_all(grad_mixed, "tensor", 0, 0, tiled=True)
    grad_attn = grad_attn.reshape(all_rows, heads * head_size)
    mixed, grad_resid_b, _ = barrier((mixed, grad_resid_b, grad_mixed))
    part_output = contract_rows(mixed, grad_resid_b).astype(BF16)
    summed_output = scattered(part_output, 1)
    mid_rows, grad_gates, grad_ups, _, _ = barrier((mid_rows, grad_gates, grad_ups, grad_mixed, part_output))
    held = []
    for give, grads in zip(gives, (grad_gates, grad_ups)):
        keep = contract_rows(mid_rows[:, :half], grads).astype(BF16)
        held.append(by_name(halving_step(keep, give, 0), relative[: dp // 2]))
    grad_attn, down_move, held = barrier((grad_attn, down_move, held))
    down_move = around((late[2] + down_move.astype(F32)).astype(BF16))
    held = [halve(held[0], bits - 1), halve(held[1], 1)]

    grad_qkv, gain_parts = backward_heads(
        qkv, grad_attn, lse, cosine, sine, gain_query, gain_key, heads, kv_heads
    )
    grad_qkv, summed_down = barrier((grad_qkv, summed_down))

    grads_in, part_pre = [], 0.0
    for k in range(parts):
        block = lax.dynamic_slice(grad_qkv, (place(k) * rows, 0), (rows, grad_qkv.shape[1]))
        grads_in.append(contract_cols(block, w_qkv))
        wide, scale = normals[k]
        part_pre = part_pre + jnp.sum(grads_in[k] * (wide * scale), axis=0)

    def gain_filler():
        packed = jnp.concatenate([part_pre, part_mid, gain_parts[0], gain_parts[1]])
        return butterfly(packed.reshape(-1, 128)).reshape(-1)

    part_qkv = contract_rows(normed_full, grad_qkv).astype(BF16)
    moves = [down_move, held]

    def first_filler():
        return part_qkv, [moves[0], summed_output]

    def second_filler():
        return gain_filler(), moves

    def down_step(k, down_move):
        return around((late[k] + down_move.astype(F32)).astype(BF16)) if k < parts else down_move

    def first_step(tied):
        down_move, summed = tied
        moves[0] = down_step(3, down_move)
        blocks = lax.all_to_all(
            summed.reshape(parts, summed.shape[0] // parts, summed.shape[1]), "tensor", 0, 0, tiled=True
        )
        moves.append(blocks)

    tied = []

    def late_filler():
        first_step(tied[0])
        return second_filler()

    grad_pre_in, made = scatter_ring(lambda k: grads_in[k], (first_filler, late_filler), tied)
    gain_sums, (down_move, held, blocks) = made[1]
    for k in range(4, parts):
        down_move = down_step(k, down_move)
    for at in range(1, bits - 1):
        held = [halve(held[0], bits - 1 - at), halve(held[1], 1 + at)]
    summed_output = jnp.sum(blocks.astype(F32), axis=0)
    summed_gate, summed_up = (h[0] for h in held)
    layer_out = (resid + late[0] + down_move.astype(F32)).astype(BF16)
    summed_qkv = scattered(part_qkv, 0).astype(F32)
    scale_pre = normals[0][1]
    back_pre = rms_back(inputs_wide * scale_pre, scale_pre, pre_full, grad_pre_in)
    in_grad = (grad_resid + back_pre).astype(BF16)

    summed_down = summed_down.astype(F32)
    summed_gate_up = jnp.stack([summed_gate.astype(F32), summed_up.astype(F32)], axis=1)
    cuts = [w_query.shape[1], w_query.shape[1] + w_key.shape[1]]
    summed_query, summed_key, summed_value = jnp.split(summed_qkv, cuts, axis=1)

    outs, at = [], 0
    for full, size in zip((width, width, head_size, head_size), sizes):
        outs.append(lax.dynamic_slice(gain_sums, (at + mine * size,), (size,)))
        at += full
    return (
        layer_out,
        in_grad,
        summed_query,
        summed_key,
        summed_value,
        summed_output,
        summed_gate_up,
        summed_down,
        *outs,
    )


def solution(mesh):
    placed = (
        P(("dp", "tensor"), None),
        P("dp", "tensor"),
        P("dp", "tensor"),
        P("dp", "tensor"),
        P("tensor", "dp"),
        P("dp", None, "tensor"),
        P("tensor", "dp"),
        P("dp"),
        P("dp"),
        P("dp"),
        P("dp"),
        P(("dp", "tensor"), None),
    )
    return jax.shard_map(
        functools.partial(on_device, (mesh.shape["dp"], mesh.shape["tensor"])),
        mesh=mesh,
        in_specs=placed,
        out_specs=(
            P(("dp", "tensor"), None),
            P(("dp", "tensor"), None),
            P("dp", "tensor"),
            P("dp", "tensor"),
            P("dp", "tensor"),
            P("tensor", "dp"),
            P("dp", None, "tensor"),
            P("tensor", "dp"),
            P("dp"),
            P("dp"),
            P("dp"),
            P("dp"),
        ),
        check_vma=False,
    )
```

```python
import functools

import jax
import jax.numpy as jnp
from jax import lax
from jax.experimental import pallas as pl
from jax.experimental.pallas import tpu as pltpu
from jax.sharding import PartitionSpec as P


L = 1024


EPS = 1e-06
THETA = 1000000.0
F32 = jnp.float32
BF16 = jnp.bfloat16
BLOCK = 256


barrier = lax.optimization_barrier


def dot(left, right):
    return jnp.dot(left, right, preferred_element_type=F32)


def contract_rows(left, right):
    return lax.dot_general(left, right, (((0,), (0,)), ((), ())), preferred_element_type=F32)


def contract_cols(left, right):
    return lax.dot_general(left, right, (((1,), (1,)), ((), ())), preferred_element_type=F32)


def rope_tables(head_size):
    half = head_size // 2
    freq = THETA ** (-(jnp.arange(half, dtype=F32) * 2.0) / head_size)
    angle = jnp.arange(L).astype(F32)[:, None] * freq[None, :]
    cosine, sine = jnp.cos(angle), jnp.sin(angle)
    return (
        jnp.concatenate([cosine, cosine], axis=1),
        jnp.concatenate([-sine, sine], axis=1),
    )


def rms_scale(values):
    return lax.rsqrt(jnp.mean(values * values, axis=-1, keepdims=True) + EPS)


def rms_back(normal, scale, gain, grads):
    scaled = grads * gain
    inner = jnp.mean(scaled * normal, axis=-1, keepdims=True)
    return scale * (scaled - normal * inner)


def turn(values):
    return pltpu.roll(values, values.shape[-1] // 2, 1)


def causal_block(scores_t):
    keys = lax.broadcasted_iota(jnp.int32, scores_t.shape, 0)
    queries = lax.broadcasted_iota(jnp.int32, scores_t.shape, 1)
    return keys <= queries


def attention_forward(group, size, q_ref, k_ref, v_ref, cos_ref, sin_ref, gq_ref, gk_ref, out_ref, lse_ref):
    cosine, sine = cos_ref[...], sin_ref[...]
    factor = size ** (-0.5)
    keys = k_ref[...]
    keys = keys * rms_scale(keys) * gk_ref[...]
    keys = (keys * cosine + turn(keys) * sine).astype(BF16)
    values_t = v_ref[...].T.astype(BF16)
    for h in range(group):
        query = q_ref[:, h * size : (h + 1) * size]
        query = query * rms_scale(query) * gq_ref[...]
        query = (query * cosine + turn(query) * sine).astype(BF16)
        for b in range(L // BLOCK):
            lo, hi = b * BLOCK, (b + 1) * BLOCK
            scores = contract_cols(keys[:hi], query[lo:hi]) * factor
            powers = jnp.exp(scores)
            last = jnp.where(causal_block(powers[lo:]), powers[lo:], 0.0)
            powers = jnp.concatenate([powers[:lo], last], axis=0) if lo else last
            total = jnp.sum(powers, axis=0, keepdims=True)
            probs = (powers * (1.0 / total)).astype(BF16)
            mixed_t = dot(values_t[:, :hi], probs)
            out_ref[lo:hi, h * size : (h + 1) * size] = mixed_t.T.astype(BF16)
            lse_ref[0, h : h + 1, lo:hi] = jnp.log(total)


def attention_backward(
    group, size, heads, kv_heads, q_ref, k_ref, v_ref, grad_ref, lse_ref, cos_ref, sin_ref, gq_ref, gk_ref,
    out_ref, gain_ref, dk_ref, dv_ref, dq_ref,
):
    first = (pl.program_id(0) == 0) & (pl.program_id(1) == 0)

    @pl.when(first)
    def _():
        gain_ref[...] = jnp.zeros_like(gain_ref)

    at = pl.program_id(1)
    cosine, sine = cos_ref[...], sin_ref[...]
    factor = size ** (-0.5)
    raw_k = k_ref[...]
    scale_k = rms_scale(raw_k)
    normal_k = raw_k * scale_k
    keys = normal_k * gk_ref[...]
    keys = keys * cosine + turn(keys) * sine
    keys_t = keys.T.astype(BF16)
    keys = keys.astype(BF16)
    values = v_ref[...].astype(BF16)
    dk_ref[...] = jnp.zeros_like(dk_ref)
    dv_ref[...] = jnp.zeros_like(dv_ref)
    for h in range(group):
        cols = slice(h * size, (h + 1) * size)
        raw_q = q_ref[:, cols]
        scale_q = rms_scale(raw_q)
        normal_q = raw_q * scale_q
        query = normal_q * gq_ref[...]
        query = (query * cosine + turn(query) * sine).astype(BF16)
        grad = grad_ref[:, cols]
        for b in range(L // BLOCK):
            lo, hi = b * BLOCK, (b + 1) * BLOCK
            q_b, g_b = query[lo:hi], grad[lo:hi]
            scores = contract_cols(keys[:hi], q_b) * factor
            probs = jnp.exp(scores - lse_ref[0, h : h + 1, lo:hi])
            last = jnp.where(causal_block(probs[lo:]), probs[lo:], 0.0)
            probs = jnp.concatenate([probs[:lo], last], axis=0) if lo else last
            dv_ref[:hi] += dot(probs.astype(BF16), g_b)
            grad_probs = contract_cols(values[:hi], g_b)
            inner = jnp.sum(probs * grad_probs, axis=0, keepdims=True)
            grad_scores = (probs * (grad_probs - inner) * factor).astype(BF16)
            dk_ref[:hi] += dot(grad_scores, q_b)
            dq_ref[lo:hi] = dot(keys_t[:, :hi], grad_scores).T
        dq = dq_ref[...]
        dqn = dq * cosine - turn(dq) * sine
        gain_ref[0:1] += jnp.sum(dqn * normal_q, axis=0, keepdims=True)
        back = rms_back(normal_q, scale_q, gq_ref[...], dqn)
        out_ref[:, pl.ds(pl.multiple_of((at * group + h) * size, size), size)] = back.astype(BF16)
    dk = dk_ref[...]
    dkn = dk * cosine - turn(dk) * sine
    gain_ref[1:2] += jnp.sum(dkn * normal_k, axis=0, keepdims=True)
    back = rms_back(normal_k, scale_k, gk_ref[...], dkn)
    out_ref[:, pl.ds(pl.multiple_of((heads + at) * size, size), size)] = back.astype(BF16)
    out_ref[:, pl.ds(pl.multiple_of((heads + kv_heads + at) * size, size), size)] = dv_ref[...].astype(BF16)


def hidden_kernel(blocks, *refs):
    gate_refs, up_refs = refs[:blocks], refs[blocks : 2 * blocks]
    mid_ref, og_ref, down_ref, hidden_ref, grad_gate_ref, grad_up_ref, back_ref, out_ref = refs[2 * blocks :]
    gate_w = jnp.concatenate([ref[...] for ref in gate_refs], axis=0)
    up_w = jnp.concatenate([ref[...] for ref in up_refs], axis=0)
    mid, down_w = mid_ref[...], down_ref[...]
    gate = dot(mid, gate_w)
    upper = dot(mid, up_w)
    grad_hidden = contract_cols(og_ref[...], down_w)
    sigma = 1.0 / (1.0 + jnp.exp(-gate))
    silu = gate * sigma
    hidden = (silu * upper).astype(BF16)
    grad_gate = (grad_hidden * upper * sigma * (1.0 + gate * (1.0 - sigma))).astype(BF16)
    grad_up = (grad_hidden * silu).astype(BF16)
    hidden_ref[...] = hidden
    grad_gate_ref[...] = grad_gate
    grad_up_ref[...] = grad_up
    back = contract_cols(grad_gate, gate_w) + contract_cols(grad_up, up_w)
    out = dot(hidden, down_w)

    @pl.when(pl.program_id(0) == 0)
    def _():
        back_ref[...] = back
        out_ref[...] = out

    @pl.when(pl.program_id(0) > 0)
    def _():
        back_ref[...] += back
        out_ref[...] += out


def hidden_piece(mid, og, gate_blocks, up_blocks, down_w):
    rows, width = mid.shape
    units = down_w.shape[0]
    blocks = len(gate_blocks)
    tile = min(512, units)
    whole = pl.BlockSpec((rows, width), lambda j: (0, 0))
    out = pl.BlockSpec((rows, tile), lambda j: (0, j))
    block = pl.BlockSpec((width // blocks, tile), lambda j: (0, j))
    return pl.pallas_call(
        functools.partial(hidden_kernel, blocks),
        grid=(units // tile,),
        in_specs=[block] * (2 * blocks) + [whole, whole, pl.BlockSpec((tile, width), lambda j: (j, 0))],
        out_specs=(out, out, out, whole, whole),
        out_shape=tuple(jax.ShapeDtypeStruct((rows, units), BF16) for _ in range(3))
        + tuple(jax.ShapeDtypeStruct((rows, width), F32) for _ in range(2)),
        cost_estimate=pl.CostEstimate(
            flops=12 * rows * width * units,
            transcendentals=rows * units,
            bytes_accessed=6 * width * units + 12 * rows * width + 6 * rows * units,
        ),
        name="hidden_piece",
    )(*gate_blocks, *up_blocks, mid, og, down_w)


def shuffle_kernel(size, order_ref, in_ref, out_ref):
    for i in range(in_ref.shape[1] // size):
        at = pl.multiple_of(order_ref[i] * size, size)
        out_ref[:, i * size : (i + 1) * size] = in_ref[:, pl.ds(at, size)]


def shuffled(values, order):
    size = values.shape[1] // order.shape[0]
    if size % 128:
        cut = values.reshape(values.shape[0], order.shape[0], size)
        return cut[:, order].reshape(values.shape)
    whole = pl.BlockSpec(values.shape, lambda i, order: (0, 0))
    return pl.pallas_call(
        functools.partial(shuffle_kernel, size),
        grid_spec=pltpu.PrefetchScalarGridSpec(
            num_scalar_prefetch=1, grid=(1,), in_specs=[whole], out_specs=whole
        ),
        out_shape=jax.ShapeDtypeStruct(values.shape, values.dtype),
        cost_estimate=pl.CostEstimate(
            flops=0, transcendentals=0, bytes_accessed=2 * values.size * values.dtype.itemsize
        ),
        name="shuffled",
    )(order, values)


def qkv_specs(group, size, heads, kv_heads):
    return [
        pl.BlockSpec((L, group * size), lambda s, g: (s, g)),
        pl.BlockSpec((L, size), lambda s, g: (s, heads + g)),
        pl.BlockSpec((L, size), lambda s, g: (s, heads + kv_heads + g)),
    ]


def forward_heads(qkv, cosine, sine, gain_q, gain_k, heads, kv_heads):
    rows, size, group = qkv.shape[0], cosine.shape[1], heads // kv_heads
    fixed = pl.BlockSpec((L, size), lambda s, g: (0, 0))
    gain = pl.BlockSpec((1, size), lambda s, g: (0, 0))
    return pl.pallas_call(
        functools.partial(attention_forward, group, size),
        grid=(rows // L, kv_heads),
        in_specs=qkv_specs(group, size, heads, kv_heads) + [fixed, fixed, gain, gain],
        out_specs=(
            pl.BlockSpec((L, group * size), lambda s, g: (s, g)),
            pl.BlockSpec((1, group, L), lambda s, g: (s * kv_heads + g, 0, 0)),
        ),
        out_shape=(
            jax.ShapeDtypeStruct((rows, heads * size), BF16),
            jax.ShapeDtypeStruct((rows // L * kv_heads, group, L), F32),
        ),
        cost_estimate=pl.CostEstimate(
            flops=4 * heads * rows * L * size,
            transcendentals=heads * rows * L,
            bytes_accessed=rows * (heads + 2 * kv_heads) * size * 4 + rows * heads * size * 2,
        ),
        name="attention_forward",
    )(qkv, qkv, qkv, cosine, sine, gain_q, gain_k)


def backward_heads(qkv, grad, lse, cosine, sine, gain_q, gain_k, heads, kv_heads):
    rows, size, group = qkv.shape[0], cosine.shape[1], heads // kv_heads
    width = (heads + 2 * kv_heads) * size
    fixed = pl.BlockSpec((L, size), lambda s, g: (0, 0))
    gain = pl.BlockSpec((1, size), lambda s, g: (0, 0))
    return pl.pallas_call(
        functools.partial(attention_backward, group, size, heads, kv_heads),
        grid=(rows // L, kv_heads),
        in_specs=qkv_specs(group, size, heads, kv_heads)
        + [
            pl.BlockSpec((L, group * size), lambda s, g: (s, g)),
            pl.BlockSpec((1, group, L), lambda s, g: (s * kv_heads + g, 0, 0)),
            fixed,
            fixed,
            gain,
            gain,
        ],
        out_specs=(
            pl.BlockSpec((L, width), lambda s, g: (s, 0)),
            pl.BlockSpec((2, size), lambda s, g: (0, 0)),
        ),
        out_shape=(
            jax.ShapeDtypeStruct((rows, width), BF16),
            jax.ShapeDtypeStruct((2, size), F32),
        ),
        scratch_shapes=[pltpu.VMEM((L, size), F32)] * 3,
        cost_estimate=pl.CostEstimate(
            flops=10 * heads * rows * L * size,
            transcendentals=heads * rows * L,
            bytes_accessed=rows * width * 6 + rows * heads * size * 2,
        ),
        name="attention_backward",
    )(qkv, qkv, qkv, grad, lse, cosine, sine, gain_q, gain_k)


def on_device(
    devices,
    layer_in,
    w_query,
    w_key,
    w_value,
    w_output,
    w_gate_up,
    w_down,
    pre_gain,
    mid_gain,
    query_gain,
    key_gain,
    out_grad,
):
    dp, parts = devices
    ring = [(i, (i + 1) % parts) for i in range(parts)]
    me = lax.axis_index("tensor")
    mine = lax.axis_index("dp")
    rows, width = layer_in.shape
    all_rows = rows * parts
    head_size = query_gain.shape[0] * dp
    heads = w_query.shape[1] // head_size
    kv_heads = w_key.shape[1] // head_size

    def place(k):
        return (me + parts - k) % parts

    def around(block):
        return lax.ppermute(block, "tensor", ring)

    def gather_ring(block):
        blocks = [block]
        for _ in range(1, parts):
            blocks.append(around(blocks[-1]))
        return blocks

    def scatter_ring(part, fillers=(), tied=None):
        order = list(range(1, parts)) + [0]
        made = []
        total = part(order[0])
        for j, k in enumerate(order[1:]):
            moving = around(total.astype(BF16))
            ahead = part(k)
            new = fillers[j]() if j < len(fillers) else ()
            moving, ahead, new = barrier((moving, ahead, new))
            total = ahead + moving.astype(F32)
            made.append(new)
            if tied is not None and isinstance(new, tuple) and len(new) > 1:
                tied.append(new[1])
        return total, made

    def scattered(part, axis):
        return lax.psum_scatter(part, "dp", scatter_dimension=axis, tiled=True)

    bits = dp.bit_length() - 1

    def swap(block, bit):
        return lax.ppermute(block, "dp", [(i, i ^ (1 << bit)) for i in range(dp)])

    near_last = list(range(1, bits)) + [0]
    relative = [0]
    for bit in near_last:
        relative = relative + [r | (1 << bit) for r in relative]

    def doubling_step(held, bit):
        return {**held, **{r | (1 << bit): swap(block, bit) for r, block in held.items()}}

    def halving_step(keep, give, bit):
        return (keep.astype(F32) + swap(give, bit).astype(F32)).astype(BF16)

    def halve(held, bit):
        keep = [r for r in held if not (r >> bit) & 1]
        far = swap(jnp.concatenate([held[r | (1 << bit)] for r in keep], axis=0), bit)
        size = far.shape[0] // len(keep)
        return {
            r: (held[r].astype(F32) + far[i * size : (i + 1) * size].astype(F32)).astype(BF16)
            for i, r in enumerate(keep)
        }

    def by_name(block, names):
        size = block.shape[0] // len(names)
        return {r: block[i * size : (i + 1) * size] for i, r in enumerate(names)}

    def butterfly(values):
        for axis, size in (("dp", dp), ("tensor", parts)):
            for bit in range(size.bit_length() - 1):
                values = values + lax.ppermute(values, axis, [(i, i ^ (1 << bit)) for i in range(size)])
        return values

    sizes = (pre_gain.shape[0], mid_gain.shape[0], query_gain.shape[0], key_gain.shape[0])
    used = sum(sizes)
    packed = jnp.concatenate([pre_gain, mid_gain, query_gain, key_gain])
    packed = jnp.pad(packed, (0, -used % 128)).reshape(1, -1)
    w_qkv = lax.all_gather(jnp.concatenate([w_query, w_key, w_value], axis=1), "dp", axis=0, tiled=True)
    xs = [layer_in, around(layer_in)]
    steps = list(zip(near_last, near_last[:-1][::-1] + near_last[-1:]))
    blocks = [{0: w_gate_up[:, 0]}, {0: w_gate_up[:, 1]}]

    def double(hop):
        if steps:
            for i, bit in enumerate(steps.pop(0)):
                blocks[i] = doubling_step(blocks[i], bit)
            blocks[:], hop = barrier((blocks, hop))
        return hop

    cosine, sine = rope_tables(head_size)
    xs[1], cosine, sine = barrier((xs[1], cosine, sine))
    w_output, packed, _ = barrier((w_output, packed, xs[1]))
    output_w = lax.all_gather(w_output, "tensor", axis=0, tiled=True)
    gains = lax.all_gather(packed, "dp", axis=0, tiled=True).astype(F32)
    starts = [sum(sizes[:i]) for i in range(5)]
    pre_full, mid_full, gain_query, gain_key = (
        gains[:, lo:hi].reshape(1, -1) for lo, hi in zip(starts, starts[1:])
    )

    normals = []
    qkv = jnp.zeros((all_rows, w_qkv.shape[1]), F32)
    normed_full = jnp.zeros((all_rows, width), BF16)
    for k in range(parts):
        if 0 < k < parts - 1:
            xs.append(around(xs[k]))
        wide = xs[k].astype(F32)
        scale = rms_scale(wide)
        normals.append((wide, scale))
        normed = (wide * scale * pre_full).astype(BF16)
        at = (place(k) * rows, 0)
        normed_full = lax.dynamic_update_slice(normed_full, normed, at)
        qkv = lax.dynamic_update_slice(qkv, dot(normed, w_qkv), at)
        if k == 1:
            xs[2] = double(xs[2])
        if k == parts - 2:
            qkv, normed_full, xs[-1], output_w = barrier((qkv, normed_full, xs[-1], output_w))
            output_w = lax.all_gather(output_w, "dp", axis=1, tiled=True)

    down_w = lax.all_gather(w_down, "dp", axis=1, tiled=True)
    first_og, _ = barrier((out_grad, xs[-1]))
    ogs = [out_grad, around(first_og)]
    attention, lse = forward_heads(qkv, cosine, sine, gain_query, gain_key, heads, kv_heads)
    attention, ogs[1] = barrier((attention, ogs[1]))
    ogs.append(around(ogs[1]))
    mixed = lax.all_to_all(
        attention.reshape(parts, rows, heads * head_size), "tensor", 0, 0, tiled=True
    )
    mixed = mixed.transpose(1, 0, 2).reshape(rows, parts * heads * head_size)
    mixed, ogs[-1] = barrier((mixed, ogs[-1]))
    while len(steps) > 1:
        mixed = double(mixed)
    for k in range(2, parts - 1):
        ogs.append(around(ogs[k]))
    inputs_wide = normals[0][0]
    resid = inputs_wide + dot(mixed, output_w)
    scale_mid = rms_scale(resid)
    normal_mid = resid * scale_mid
    mids = gather_ring(
        shuffled((normal_mid * mid_full).astype(BF16), mine ^ jnp.asarray(relative, jnp.int32))
    )
    if parts > 1:
        mids[1] = double(mids[1])
    gate_blocks, up_blocks = ([held[r] for r in relative] for held in blocks)
    pieces = {}

    def piece(k):
        pieces[k] = hidden_piece(mids[k], ogs[k], gate_blocks, up_blocks, down_w)
        return pieces[k][3]

    def rows_of(blocks):
        return jnp.concatenate(blocks, axis=0)

    def column(i):
        return rows_of([pieces[k][i] for k in range(parts)])

    half = width // 2
    piece(1)
    down_parts = []

    def down_filler():
        down_parts.append(contract_rows(column(0), rows_of(ogs)).astype(BF16))
        return down_parts[0]

    grad_mid_in, _ = scatter_ring(piece, [tuple] * (parts - 2) + [down_filler])
    summed_down = scattered(down_parts[0], 1)
    mid_rows, grad_gates, grad_ups = rows_of(mids), column(1), column(2)
    gives = [contract_rows(mid_rows[:, half:], grads).astype(BF16) for grads in (grad_gates, grad_ups)]
    back_order = [relative.index(r) for r in range(dp)]
    late = [pieces[k][4] for k in range(parts)]
    down_move, grad_mid_in = barrier((late[1].astype(BF16), grad_mid_in))
    down_move = around(down_move)
    late = barrier((late, grad_mid_in))[0]
    grad_mid_in = shuffled(
        grad_mid_in, jnp.asarray(back_order, jnp.int32)[mine ^ jnp.arange(dp, dtype=jnp.int32)]
    )
    grad_resid = out_grad.astype(F32) + rms_back(normal_mid, scale_mid, mid_full, grad_mid_in)
    part_mid = jnp.sum(grad_mid_in * normal_mid, axis=0)
    grad_resid_b = grad_resid.astype(BF16)

    grad_mixed = contract_cols(grad_resid_b, output_w).astype(BF16)
    grad_mixed = grad_mixed.reshape(rows, parts, heads * head_size).transpose(1, 0, 2)
    grad_attn = lax.all_to_all(grad_mixed, "tensor", 0, 0, tiled=True)
    grad_attn = grad_attn.reshape(all_rows, heads * head_size)
    mixed, grad_resid_b, _ = barrier((mixed, grad_resid_b, grad_mixed))
    part_output = contract_rows(mixed, grad_resid_b).astype(BF16)
    summed_output = scattered(part_output, 1)
    mid_rows, grad_gates, grad_ups, _, _ = barrier((mid_rows, grad_gates, grad_ups, grad_mixed, part_output))
    held = []
    for give, grads in zip(gives, (grad_gates, grad_ups)):
        keep = contract_rows(mid_rows[:, :half], grads).astype(BF16)
        held.append(by_name(halving_step(keep, give, 0), relative[: dp // 2]))
    grad_attn, down_move, held = barrier((grad_attn, down_move, held))
    down_move = around((late[2] + down_move.astype(F32)).astype(BF16))
    held = [halve(held[0], bits - 1), halve(held[1], 1)]

    grad_qkv, gain_parts = backward_heads(
        qkv, grad_attn, lse, cosine, sine, gain_query, gain_key, heads, kv_heads
    )
    grad_qkv, summed_down = barrier((grad_qkv, summed_down))

    grads_in, part_pre = [], 0.0
    for k in range(parts):
        block = lax.dynamic_slice(grad_qkv, (place(k) * rows, 0), (rows, grad_qkv.shape[1]))
        grads_in.append(contract_cols(block, w_qkv))
        wide, scale = normals[k]
        part_pre = part_pre + jnp.sum(grads_in[k] * (wide * scale), axis=0)

    def gain_filler():
        packed = jnp.concatenate([part_pre, part_mid, gain_parts[0], gain_parts[1]])
        packed = barrier((packed, tied[0][0]))[0]
        return butterfly(packed.reshape(-1, 128)).reshape(-1)

    part_qkv = contract_rows(normed_full, grad_qkv).astype(BF16)
    moves = [down_move, held]

    def first_filler():
        return part_qkv, [moves[0], summed_output]

    def second_filler():
        return gain_filler(), moves

    def down_step(k, down_move):
        return around((late[k] + down_move.astype(F32)).astype(BF16)) if k < parts else down_move

    def first_step(tied):
        down_move, summed = tied
        moves[0] = down_step(3, down_move)
        blocks = lax.all_to_all(
            summed.reshape(parts, summed.shape[0] // parts, summed.shape[1]), "tensor", 0, 0, tiled=True
        )
        moves.append(blocks)

    tied = []

    def late_filler():
        first_step(tied[0])
        return second_filler()

    grad_pre_in, made = scatter_ring(lambda k: grads_in[k], (first_filler, late_filler), tied)
    gain_sums, (down_move, held, blocks) = made[1]
    for k in range(4, parts):
        down_move = down_step(k, down_move)
    for at in range(1, bits - 1):
        held = [halve(held[0], bits - 1 - at), halve(held[1], 1 + at)]
    summed_output = jnp.sum(blocks.astype(F32), axis=0)
    summed_gate, summed_up = (h[0] for h in held)
    layer_out = (resid + late[0] + down_move.astype(F32)).astype(BF16)
    summed_qkv = scattered(part_qkv, 0).astype(F32)
    scale_pre = normals[0][1]
    back_pre = rms_back(inputs_wide * scale_pre, scale_pre, pre_full, grad_pre_in)
    in_grad = (grad_resid + back_pre).astype(BF16)

    summed_down = summed_down.astype(F32)
    summed_gate_up = jnp.stack([summed_gate.astype(F32), summed_up.astype(F32)], axis=1)
    cuts = [w_query.shape[1], w_query.shape[1] + w_key.shape[1]]
    summed_query, summed_key, summed_value = jnp.split(summed_qkv, cuts, axis=1)

    outs, at = [], 0
    for full, size in zip((width, width, head_size, head_size), sizes):
        outs.append(lax.dynamic_slice(gain_sums, (at + mine * size,), (size,)))
        at += full
    return (
        layer_out,
        in_grad,
        summed_query,
        summed_key,
        summed_value,
        summed_output,
        summed_gate_up,
        summed_down,
        *outs,
    )


def solution(mesh):
    placed = (
        P(("dp", "tensor"), None),
        P("dp", "tensor"),
        P("dp", "tensor"),
        P("dp", "tensor"),
        P("tensor", "dp"),
        P("dp", None, "tensor"),
        P("tensor", "dp"),
        P("dp"),
        P("dp"),
        P("dp"),
        P("dp"),
        P(("dp", "tensor"), None),
    )
    return jax.shard_map(
        functools.partial(on_device, (mesh.shape["dp"], mesh.shape["tensor"])),
        mesh=mesh,
        in_specs=placed,
        out_specs=(
            P(("dp", "tensor"), None),
            P(("dp", "tensor"), None),
            P("dp", "tensor"),
            P("dp", "tensor"),
            P("dp", "tensor"),
            P("tensor", "dp"),
            P("dp", None, "tensor"),
            P("tensor", "dp"),
            P("dp"),
            P("dp"),
            P("dp"),
            P("dp"),
        ),
        check_vma=False,
    )
```

```python
import functools

import jax
import jax.numpy as jnp
from jax import lax
from jax.experimental import pallas as pl
from jax.experimental.pallas import tpu as pltpu
from jax.sharding import PartitionSpec as P


L = 1024


EPS = 1e-06
THETA = 1000000.0
F32 = jnp.float32
BF16 = jnp.bfloat16
BLOCK = 256


barrier = lax.optimization_barrier


def dot(left, right):
    return jnp.dot(left, right, preferred_element_type=F32)


def contract_rows(left, right):
    return lax.dot_general(left, right, (((0,), (0,)), ((), ())), preferred_element_type=F32)


def contract_cols(left, right):
    return lax.dot_general(left, right, (((1,), (1,)), ((), ())), preferred_element_type=F32)


def rope_tables(head_size):
    half = head_size // 2
    freq = THETA ** (-(jnp.arange(half, dtype=F32) * 2.0) / head_size)
    angle = jnp.arange(L).astype(F32)[:, None] * freq[None, :]
    cosine, sine = jnp.cos(angle), jnp.sin(angle)
    return (
        jnp.concatenate([cosine, cosine], axis=1),
        jnp.concatenate([-sine, sine], axis=1),
    )


def rms_scale(values):
    return lax.rsqrt(jnp.mean(values * values, axis=-1, keepdims=True) + EPS)


def rms_back(normal, scale, gain, grads):
    scaled = grads * gain
    inner = jnp.mean(scaled * normal, axis=-1, keepdims=True)
    return scale * (scaled - normal * inner)


def turn(values):
    return pltpu.roll(values, values.shape[-1] // 2, 1)


def causal_block(scores_t):
    keys = lax.broadcasted_iota(jnp.int32, scores_t.shape, 0)
    queries = lax.broadcasted_iota(jnp.int32, scores_t.shape, 1)
    return keys <= queries


def attention_forward(group, size, q_ref, k_ref, v_ref, cos_ref, sin_ref, gq_ref, gk_ref, out_ref, lse_ref):
    cosine, sine = cos_ref[...], sin_ref[...]
    factor = size ** (-0.5)
    keys = k_ref[...]
    keys = keys * rms_scale(keys) * gk_ref[...]
    keys = (keys * cosine + turn(keys) * sine).astype(BF16)
    values_t = v_ref[...].T.astype(BF16)
    for h in range(group):
        query = q_ref[:, h * size : (h + 1) * size]
        query = query * rms_scale(query) * gq_ref[...]
        query = (query * cosine + turn(query) * sine).astype(BF16)
        for b in range(L // BLOCK):
            lo, hi = b * BLOCK, (b + 1) * BLOCK
            scores = contract_cols(keys[:hi], query[lo:hi]) * factor
            powers = jnp.exp(scores)
            last = jnp.where(causal_block(powers[lo:]), powers[lo:], 0.0)
            powers = jnp.concatenate([powers[:lo], last], axis=0) if lo else last
            total = jnp.sum(powers, axis=0, keepdims=True)
            probs = (powers * (1.0 / total)).astype(BF16)
            mixed_t = dot(values_t[:, :hi], probs)
            out_ref[lo:hi, h * size : (h + 1) * size] = mixed_t.T.astype(BF16)
            lse_ref[0, h : h + 1, lo:hi] = jnp.log(total)


def attention_backward(
    group, size, heads, kv_heads, q_ref, k_ref, v_ref, grad_ref, lse_ref, cos_ref, sin_ref, gq_ref, gk_ref,
    out_ref, gain_ref, dk_ref, dv_ref, dq_ref,
):
    first = (pl.program_id(0) == 0) & (pl.program_id(1) == 0)

    @pl.when(first)
    def _():
        gain_ref[...] = jnp.zeros_like(gain_ref)

    at = pl.program_id(1)
    cosine, sine = cos_ref[...], sin_ref[...]
    factor = size ** (-0.5)
    raw_k = k_ref[...]
    scale_k = rms_scale(raw_k)
    normal_k = raw_k * scale_k
    keys = normal_k * gk_ref[...]
    keys = keys * cosine + turn(keys) * sine
    keys_t = keys.T.astype(BF16)
    keys = keys.astype(BF16)
    values = v_ref[...].astype(BF16)
    dk_ref[...] = jnp.zeros_like(dk_ref)
    dv_ref[...] = jnp.zeros_like(dv_ref)
    for h in range(group):
        cols = slice(h * size, (h + 1) * size)
        raw_q = q_ref[:, cols]
        scale_q = rms_scale(raw_q)
        normal_q = raw_q * scale_q
        query = normal_q * gq_ref[...]
        query = (query * cosine + turn(query) * sine).astype(BF16)
        grad = grad_ref[:, cols]
        for b in range(L // BLOCK):
            lo, hi = b * BLOCK, (b + 1) * BLOCK
            q_b, g_b = query[lo:hi], grad[lo:hi]
            scores = contract_cols(keys[:hi], q_b) * factor
            probs = jnp.exp(scores - lse_ref[0, h : h + 1, lo:hi])
            last = jnp.where(causal_block(probs[lo:]), probs[lo:], 0.0)
            probs = jnp.concatenate([probs[:lo], last], axis=0) if lo else last
            dv_ref[:hi] += dot(probs.astype(BF16), g_b)
            grad_probs = contract_cols(values[:hi], g_b)
            inner = jnp.sum(probs * grad_probs, axis=0, keepdims=True)
            grad_scores = (probs * (grad_probs - inner) * factor).astype(BF16)
            dk_ref[:hi] += dot(grad_scores, q_b)
            dq_ref[lo:hi] = dot(keys_t[:, :hi], grad_scores).T
        dq = dq_ref[...]
        dqn = dq * cosine - turn(dq) * sine
        gain_ref[0:1] += jnp.sum(dqn * normal_q, axis=0, keepdims=True)
        back = rms_back(normal_q, scale_q, gq_ref[...], dqn)
        out_ref[:, pl.ds(pl.multiple_of((at * group + h) * size, size), size)] = back.astype(BF16)
    dk = dk_ref[...]
    dkn = dk * cosine - turn(dk) * sine
    gain_ref[1:2] += jnp.sum(dkn * normal_k, axis=0, keepdims=True)
    back = rms_back(normal_k, scale_k, gk_ref[...], dkn)
    out_ref[:, pl.ds(pl.multiple_of((heads + at) * size, size), size)] = back.astype(BF16)
    out_ref[:, pl.ds(pl.multiple_of((heads + kv_heads + at) * size, size), size)] = dv_ref[...].astype(BF16)


def hidden_kernel(blocks, *refs):
    gate_refs, up_refs = refs[:blocks], refs[blocks : 2 * blocks]
    mid_ref, og_ref, down_ref, hidden_ref, grad_gate_ref, grad_up_ref, back_ref, out_ref = refs[2 * blocks :]
    gate_w = jnp.concatenate([ref[...] for ref in gate_refs], axis=0)
    up_w = jnp.concatenate([ref[...] for ref in up_refs], axis=0)
    mid, down_w = mid_ref[...], down_ref[...]
    gate = dot(mid, gate_w)
    upper = dot(mid, up_w)
    grad_hidden = contract_cols(og_ref[...], down_w)
    sigma = 1.0 / (1.0 + jnp.exp(-gate))
    silu = gate * sigma
    hidden = (silu * upper).astype(BF16)
    grad_gate = (grad_hidden * upper * sigma * (1.0 + gate * (1.0 - sigma))).astype(BF16)
    grad_up = (grad_hidden * silu).astype(BF16)
    hidden_ref[...] = hidden
    grad_gate_ref[...] = grad_gate
    grad_up_ref[...] = grad_up
    back = contract_cols(grad_gate, gate_w) + contract_cols(grad_up, up_w)
    out = dot(hidden, down_w)

    @pl.when(pl.program_id(0) == 0)
    def _():
        back_ref[...] = back
        out_ref[...] = out

    @pl.when(pl.program_id(0) > 0)
    def _():
        back_ref[...] += back
        out_ref[...] += out


def hidden_piece(mid, og, gate_blocks, up_blocks, down_w):
    rows, width = mid.shape
    units = down_w.shape[0]
    blocks = len(gate_blocks)
    tile = min(512, units)
    whole = pl.BlockSpec((rows, width), lambda j: (0, 0))
    out = pl.BlockSpec((rows, tile), lambda j: (0, j))
    block = pl.BlockSpec((width // blocks, tile), lambda j: (0, j))
    return pl.pallas_call(
        functools.partial(hidden_kernel, blocks),
        grid=(units // tile,),
        in_specs=[block] * (2 * blocks) + [whole, whole, pl.BlockSpec((tile, width), lambda j: (j, 0))],
        out_specs=(out, out, out, whole, whole),
        out_shape=tuple(jax.ShapeDtypeStruct((rows, units), BF16) for _ in range(3))
        + tuple(jax.ShapeDtypeStruct((rows, width), F32) for _ in range(2)),
        cost_estimate=pl.CostEstimate(
            flops=12 * rows * width * units,
            transcendentals=rows * units,
            bytes_accessed=6 * width * units + 12 * rows * width + 6 * rows * units,
        ),
        name="hidden_piece",
    )(*gate_blocks, *up_blocks, mid, og, down_w)


def shuffle_kernel(size, order_ref, in_ref, out_ref):
    for i in range(in_ref.shape[1] // size):
        at = pl.multiple_of(order_ref[i] * size, size)
        out_ref[:, i * size : (i + 1) * size] = in_ref[:, pl.ds(at, size)]


def shuffled(values, order):
    size = values.shape[1] // order.shape[0]
    if size % 128:
        cut = values.reshape(values.shape[0], order.shape[0], size)
        return cut[:, order].reshape(values.shape)
    whole = pl.BlockSpec(values.shape, lambda i, order: (0, 0))
    return pl.pallas_call(
        functools.partial(shuffle_kernel, size),
        grid_spec=pltpu.PrefetchScalarGridSpec(
            num_scalar_prefetch=1, grid=(1,), in_specs=[whole], out_specs=whole
        ),
        out_shape=jax.ShapeDtypeStruct(values.shape, values.dtype),
        cost_estimate=pl.CostEstimate(
            flops=0, transcendentals=0, bytes_accessed=2 * values.size * values.dtype.itemsize
        ),
        name="shuffled",
    )(order, values)


def qkv_specs(group, size, heads, kv_heads):
    return [
        pl.BlockSpec((L, group * size), lambda s, g: (s, g)),
        pl.BlockSpec((L, size), lambda s, g: (s, heads + g)),
        pl.BlockSpec((L, size), lambda s, g: (s, heads + kv_heads + g)),
    ]


def forward_heads(qkv, cosine, sine, gain_q, gain_k, heads, kv_heads):
    rows, size, group = qkv.shape[0], cosine.shape[1], heads // kv_heads
    fixed = pl.BlockSpec((L, size), lambda s, g: (0, 0))
    gain = pl.BlockSpec((1, size), lambda s, g: (0, 0))
    return pl.pallas_call(
        functools.partial(attention_forward, group, size),
        grid=(rows // L, kv_heads),
        in_specs=qkv_specs(group, size, heads, kv_heads) + [fixed, fixed, gain, gain],
        out_specs=(
            pl.BlockSpec((L, group * size), lambda s, g: (s, g)),
            pl.BlockSpec((1, group, L), lambda s, g: (s * kv_heads + g, 0, 0)),
        ),
        out_shape=(
            jax.ShapeDtypeStruct((rows, heads * size), BF16),
            jax.ShapeDtypeStruct((rows // L * kv_heads, group, L), F32),
        ),
        cost_estimate=pl.CostEstimate(
            flops=4 * heads * rows * L * size,
            transcendentals=heads * rows * L,
            bytes_accessed=rows * (heads + 2 * kv_heads) * size * 4 + rows * heads * size * 2,
        ),
        name="attention_forward",
    )(qkv, qkv, qkv, cosine, sine, gain_q, gain_k)


def backward_heads(qkv, grad, lse, cosine, sine, gain_q, gain_k, heads, kv_heads):
    rows, size, group = qkv.shape[0], cosine.shape[1], heads // kv_heads
    width = (heads + 2 * kv_heads) * size
    fixed = pl.BlockSpec((L, size), lambda s, g: (0, 0))
    gain = pl.BlockSpec((1, size), lambda s, g: (0, 0))
    return pl.pallas_call(
        functools.partial(attention_backward, group, size, heads, kv_heads),
        grid=(rows // L, kv_heads),
        in_specs=qkv_specs(group, size, heads, kv_heads)
        + [
            pl.BlockSpec((L, group * size), lambda s, g: (s, g)),
            pl.BlockSpec((1, group, L), lambda s, g: (s * kv_heads + g, 0, 0)),
            fixed,
            fixed,
            gain,
            gain,
        ],
        out_specs=(
            pl.BlockSpec((L, width), lambda s, g: (s, 0)),
            pl.BlockSpec((2, size), lambda s, g: (0, 0)),
        ),
        out_shape=(
            jax.ShapeDtypeStruct((rows, width), BF16),
            jax.ShapeDtypeStruct((2, size), F32),
        ),
        scratch_shapes=[pltpu.VMEM((L, size), F32)] * 3,
        cost_estimate=pl.CostEstimate(
            flops=10 * heads * rows * L * size,
            transcendentals=heads * rows * L,
            bytes_accessed=rows * width * 6 + rows * heads * size * 2,
        ),
        name="attention_backward",
    )(qkv, qkv, qkv, grad, lse, cosine, sine, gain_q, gain_k)


def on_device(
    devices,
    layer_in,
    w_query,
    w_key,
    w_value,
    w_output,
    w_gate_up,
    w_down,
    pre_gain,
    mid_gain,
    query_gain,
    key_gain,
    out_grad,
):
    dp, parts = devices
    ring = [(i, (i + 1) % parts) for i in range(parts)]
    me = lax.axis_index("tensor")
    mine = lax.axis_index("dp")
    rows, width = layer_in.shape
    all_rows = rows * parts
    head_size = query_gain.shape[0] * dp
    heads = w_query.shape[1] // head_size
    kv_heads = w_key.shape[1] // head_size

    def place(k):
        return (me + parts - k) % parts

    def around(block):
        return lax.ppermute(block, "tensor", ring)

    def gather_ring(block):
        blocks = [block]
        for _ in range(1, parts):
            blocks.append(around(blocks[-1]))
        return blocks

    def scatter_ring(part, fillers=(), tied=None):
        order = list(range(1, parts)) + [0]
        made = []
        total = part(order[0])
        for j, k in enumerate(order[1:]):
            moving = around(total.astype(BF16))
            ahead = part(k)
            new = fillers[j]() if j < len(fillers) else ()
            moving, ahead, new = barrier((moving, ahead, new))
            total = ahead + moving.astype(F32)
            made.append(new)
            if tied is not None and isinstance(new, tuple) and len(new) > 1:
                tied.append(new[1])
        return total, made

    def scattered(part, axis):
        return lax.psum_scatter(part, "dp", scatter_dimension=axis, tiled=True)

    bits = dp.bit_length() - 1

    def swap(block, bit):
        return lax.ppermute(block, "dp", [(i, i ^ (1 << bit)) for i in range(dp)])

    near_last = list(range(1, bits)) + [0]
    relative = [0]
    for bit in near_last:
        relative = relative + [r | (1 << bit) for r in relative]

    def doubling_step(held, bit):
        return {**held, **{r | (1 << bit): swap(block, bit) for r, block in held.items()}}

    def halving_step(keep, give, bit):
        return (keep.astype(F32) + swap(give, bit).astype(F32)).astype(BF16)

    def halve(held, bit):
        keep = [r for r in held if not (r >> bit) & 1]
        far = swap(jnp.concatenate([held[r | (1 << bit)] for r in keep], axis=0), bit)
        size = far.shape[0] // len(keep)
        return {
            r: (held[r].astype(F32) + far[i * size : (i + 1) * size].astype(F32)).astype(BF16)
            for i, r in enumerate(keep)
        }

    def by_name(block, names):
        size = block.shape[0] // len(names)
        return {r: block[i * size : (i + 1) * size] for i, r in enumerate(names)}

    def butterfly(values):
        for axis, size in (("dp", dp), ("tensor", parts)):
            for bit in range(size.bit_length() - 1):
                values = values + lax.ppermute(values, axis, [(i, i ^ (1 << bit)) for i in range(size)])
        return values

    sizes = (pre_gain.shape[0], mid_gain.shape[0], query_gain.shape[0], key_gain.shape[0])
    used = sum(sizes)
    packed = jnp.concatenate([pre_gain, mid_gain, query_gain, key_gain])
    packed = jnp.pad(packed, (0, -used % 128)).reshape(1, -1)
    w_qkv = lax.all_gather(jnp.concatenate([w_query, w_key, w_value], axis=1), "dp", axis=0, tiled=True)
    xs = [layer_in, around(layer_in)]
    steps = list(zip(near_last, near_last[:-1][::-1] + near_last[-1:]))
    blocks = [{0: w_gate_up[:, 0]}, {0: w_gate_up[:, 1]}]

    def double(hop):
        if steps:
            for i, bit in enumerate(steps.pop(0)):
                blocks[i] = doubling_step(blocks[i], bit)
            blocks[:], hop = barrier((blocks, hop))
        return hop

    cosine, sine = rope_tables(head_size)
    xs[1], cosine, sine = barrier((xs[1], cosine, sine))
    w_output, packed, _ = barrier((w_output, packed, xs[1]))
    output_w = lax.all_gather(w_output, "tensor", axis=0, tiled=True)
    gains = lax.all_gather(packed, "dp", axis=0, tiled=True).astype(F32)
    starts = [sum(sizes[:i]) for i in range(5)]
    pre_full, mid_full, gain_query, gain_key = (
        gains[:, lo:hi].reshape(1, -1) for lo, hi in zip(starts, starts[1:])
    )

    normals = []
    qkv = jnp.zeros((all_rows, w_qkv.shape[1]), F32)
    normed_full = jnp.zeros((all_rows, width), BF16)
    for k in range(parts):
        if 0 < k < parts - 1:
            xs.append(around(xs[k]))
        wide = xs[k].astype(F32)
        scale = rms_scale(wide)
        normals.append((wide, scale))
        normed = (wide * scale * pre_full).astype(BF16)
        at = (place(k) * rows, 0)
        normed_full = lax.dynamic_update_slice(normed_full, normed, at)
        qkv = lax.dynamic_update_slice(qkv, dot(normed, w_qkv), at)
        if k == 1:
            xs[2] = double(xs[2])
        if k == parts - 2:
            qkv, normed_full, xs[-1], output_w = barrier((qkv, normed_full, xs[-1], output_w))
            output_w = lax.all_gather(output_w, "dp", axis=1, tiled=True)

    down_w = lax.all_gather(w_down, "dp", axis=1, tiled=True)
    first_og, _ = barrier((out_grad, xs[-1]))
    ogs = [out_grad, around(first_og)]
    attention, lse = forward_heads(qkv, cosine, sine, gain_query, gain_key, heads, kv_heads)
    attention, ogs[1] = barrier((attention, ogs[1]))
    ogs.append(around(ogs[1]))
    mixed = lax.all_to_all(
        attention.reshape(parts, rows, heads * head_size), "tensor", 0, 0, tiled=True
    )
    mixed = mixed.transpose(1, 0, 2).reshape(rows, parts * heads * head_size)
    mixed, ogs[-1] = barrier((mixed, ogs[-1]))
    while len(steps) > 1:
        mixed = double(mixed)
    for k in range(2, parts - 1):
        ogs.append(around(ogs[k]))
    inputs_wide = normals[0][0]
    resid = inputs_wide + dot(mixed, output_w)
    scale_mid = rms_scale(resid)
    normal_mid = resid * scale_mid
    mids = gather_ring(
        shuffled((normal_mid * mid_full).astype(BF16), mine ^ jnp.asarray(relative, jnp.int32))
    )
    if parts > 1:
        mids[1] = double(mids[1])
    gate_blocks, up_blocks = ([held[r] for r in relative] for held in blocks)
    pieces = {}

    def piece(k):
        pieces[k] = hidden_piece(mids[k], ogs[k], gate_blocks, up_blocks, down_w)
        return pieces[k][3]

    def rows_of(blocks):
        return jnp.concatenate(blocks, axis=0)

    def column(i):
        return rows_of([pieces[k][i] for k in range(parts)])

    half = width // 2
    piece(1)
    down_parts = []

    def down_filler():
        down_parts.append(contract_rows(column(0), rows_of(ogs)).astype(BF16))
        return down_parts[0]

    grad_mid_in, _ = scatter_ring(piece, [tuple] * (parts - 2) + [down_filler])
    summed_down = scattered(down_parts[0], 1)
    mid_rows, grad_gates, grad_ups = rows_of(mids), column(1), column(2)
    gives = [contract_rows(mid_rows[:, half:], grads).astype(BF16) for grads in (grad_gates, grad_ups)]
    back_order = [relative.index(r) for r in range(dp)]
    late = [pieces[k][4] for k in range(parts)]
    down_move, grad_mid_in = barrier((late[1].astype(BF16), grad_mid_in))
    down_move = around(down_move)
    late = barrier((late, grad_mid_in))[0]
    grad_mid_in = shuffled(
        grad_mid_in, jnp.asarray(back_order, jnp.int32)[mine ^ jnp.arange(dp, dtype=jnp.int32)]
    )
    grad_resid = out_grad.astype(F32) + rms_back(normal_mid, scale_mid, mid_full, grad_mid_in)
    part_mid = jnp.sum(grad_mid_in * normal_mid, axis=0)
    grad_resid_b = grad_resid.astype(BF16)

    grad_mixed = contract_cols(grad_resid_b, output_w).astype(BF16)
    grad_mixed = grad_mixed.reshape(rows, parts, heads * head_size).transpose(1, 0, 2)
    grad_attn = lax.all_to_all(grad_mixed, "tensor", 0, 0, tiled=True)
    grad_attn = grad_attn.reshape(all_rows, heads * head_size)
    mixed, grad_resid_b, _ = barrier((mixed, grad_resid_b, grad_mixed))
    part_output = contract_rows(mixed, grad_resid_b).astype(BF16)
    summed_output = scattered(part_output, 1)
    mid_rows, grad_gates, grad_ups, _, _ = barrier((mid_rows, grad_gates, grad_ups, grad_mixed, part_output))
    held = []
    for give, grads in zip(gives, (grad_gates, grad_ups)):
        keep = contract_rows(mid_rows[:, :half], grads).astype(BF16)
        held.append(by_name(halving_step(keep, give, 0), relative[: dp // 2]))
    grad_attn, down_move, held = barrier((grad_attn, down_move, held))
    down_move = around((late[2] + down_move.astype(F32)).astype(BF16))
    held = [halve(held[0], bits - 1), halve(held[1], 1)]

    grad_qkv, gain_parts = backward_heads(
        qkv, grad_attn, lse, cosine, sine, gain_query, gain_key, heads, kv_heads
    )
    grad_qkv, summed_down = barrier((grad_qkv, summed_down))

    grads_in, part_pre = [], 0.0
    for k in range(parts):
        block = lax.dynamic_slice(grad_qkv, (place(k) * rows, 0), (rows, grad_qkv.shape[1]))
        grads_in.append(contract_cols(block, w_qkv))
        wide, scale = normals[k]
        part_pre = part_pre + jnp.sum(grads_in[k] * (wide * scale), axis=0)

    def gain_filler():
        packed = jnp.concatenate([part_pre, part_mid, gain_parts[0], gain_parts[1]])
        packed = barrier((packed, tied[0][0]))[0]
        return butterfly(packed.reshape(-1, 128)).reshape(-1)

    part_qkv = contract_rows(normed_full, grad_qkv).astype(BF16)
    moves = [down_move, held]

    def first_filler():
        return part_qkv, [moves[0]]

    def second_filler():
        return gain_filler(), moves

    def down_step(k, down_move):
        return around((late[k] + down_move.astype(F32)).astype(BF16)) if k < parts else down_move

    tied = []

    def late_filler():
        moves[0] = down_step(3, tied[0][0])
        moves.append(summed_output)
        return second_filler()

    grad_pre_in, made = scatter_ring(lambda k: grads_in[k], (first_filler, late_filler), tied)
    gain_sums, (down_move, held, summed_output) = made[1]
    blocks = summed_output.reshape(parts, summed_output.shape[0] // parts, summed_output.shape[1])
    blocks = lax.all_to_all(blocks, "tensor", 0, 0, tiled=True)
    for k in range(4, parts):
        down_move = down_step(k, down_move)
    for at in range(1, bits - 1):
        held = [halve(held[0], bits - 1 - at), halve(held[1], 1 + at)]
    summed_output = jnp.sum(blocks.astype(F32), axis=0)
    summed_gate, summed_up = (h[0] for h in held)
    layer_out = (resid + late[0] + down_move.astype(F32)).astype(BF16)
    summed_qkv = scattered(part_qkv, 0).astype(F32)
    scale_pre = normals[0][1]
    back_pre = rms_back(inputs_wide * scale_pre, scale_pre, pre_full, grad_pre_in)
    in_grad = (grad_resid + back_pre).astype(BF16)

    summed_down = summed_down.astype(F32)
    summed_gate_up = jnp.stack([summed_gate.astype(F32), summed_up.astype(F32)], axis=1)
    cuts = [w_query.shape[1], w_query.shape[1] + w_key.shape[1]]
    summed_query, summed_key, summed_value = jnp.split(summed_qkv, cuts, axis=1)

    outs, at = [], 0
    for full, size in zip((width, width, head_size, head_size), sizes):
        outs.append(lax.dynamic_slice(gain_sums, (at + mine * size,), (size,)))
        at += full
    return (
        layer_out,
        in_grad,
        summed_query,
        summed_key,
        summed_value,
        summed_output,
        summed_gate_up,
        summed_down,
        *outs,
    )


def solution(mesh):
    placed = (
        P(("dp", "tensor"), None),
        P("dp", "tensor"),
        P("dp", "tensor"),
        P("dp", "tensor"),
        P("tensor", "dp"),
        P("dp", None, "tensor"),
        P("tensor", "dp"),
        P("dp"),
        P("dp"),
        P("dp"),
        P("dp"),
        P(("dp", "tensor"), None),
    )
    return jax.shard_map(
        functools.partial(on_device, (mesh.shape["dp"], mesh.shape["tensor"])),
        mesh=mesh,
        in_specs=placed,
        out_specs=(
            P(("dp", "tensor"), None),
            P(("dp", "tensor"), None),
            P("dp", "tensor"),
            P("dp", "tensor"),
            P("dp", "tensor"),
            P("tensor", "dp"),
            P("dp", None, "tensor"),
            P("tensor", "dp"),
            P("dp"),
            P("dp"),
            P("dp"),
            P("dp"),
        ),
        check_vma=False,
    )
```
